32 devices in a mesh: tile: 8 (over z, x), grp: 4 (over y, core).
Axes of the slice: x: 2, y: 2, z: 4, core: 2. Of those that a mesh axis runs over, the one named last changes fastest.
Arguments:
- pixels: bfloat16 [8192, 432], P(('tile', 'grp')), may hold values from -25 to 25
- labels: int32 [8192], P(('tile', 'grp')), may hold values from 0 to 63, as said below
- targets: bfloat16 [512, 432], P('grp'), may hold values from -6 to 6
Outputs:
- scores: bfloat16 [8192, 512], P(('tile', 'grp'))
The draws below stay inside these ranges and needn't reach their ends.
Inputs may be any that keep to these rules, and one draw needn't show every extreme that they name: `labels`: among the 256 pixels of each aligned block (rows b * 256 to (b + 1) * 256 - 1) no cluster occurs more than 8 times; in every draw one cluster occurs exactly 8 times in every block.
All inputs are finite; a program needn't handle non-finite values.
Results may differ from the reference program's by a relative error of at most 0.0024.
Values may be sent and summed in bfloat16 or wider, within the bound.
A program may use at most 128 MiB of HBM per device.

```python
import jax
import jax.numpy as jnp
from jax import lax

B = 432
NT = 512
NCLUST = 64
R = 256
CAP = 8
NBLK = 32


def label_table(key):
    keys = jax.random.split(jax.random.fold_in(key, 11), 4)
    common = jax.random.randint(keys[0], (), 0, NCLUST)
    extra = jax.random.randint(keys[1], (NBLK,), 0, NCLUST - 1)
    extra = extra + (extra >= common).astype(jnp.int32)
    slot_cluster = jnp.arange(NCLUST * CAP, dtype=jnp.int32) // CAP
    ranks = jax.vmap(lambda k: jax.random.permutation(k, NCLUST * CAP))(jax.random.split(keys[2], NBLK))
    ranks = ranks.astype(jnp.int32)
    priority = jnp.where(slot_cluster[None, :] == common, -2, jnp.where(slot_cluster[None, :] == extra[:, None], -1, ranks))
    order = jnp.argsort(priority, axis=1, stable=True)[:, :R]
    chosen = (order // CAP).astype(jnp.int32)
    shuffle = jax.vmap(lambda k: jax.random.permutation(k, R))(jax.random.split(keys[3], NBLK))
    chosen = jnp.take_along_axis(chosen, shuffle.astype(jnp.int32), axis=1)
    return chosen.reshape(NBLK * R).astype(jnp.int32)


def draw_labels(key, part):
    return label_table(key)


def draw_pixels(key, part):
    labels = label_table(key)
    keys = jax.random.split(jax.random.fold_in(key, 23), 3)
    means = jax.random.truncated_normal(keys[0], -3.0, 3.0, (NCLUST, B), jnp.float32)
    spread = jnp.exp(jax.random.uniform(keys[1], (NCLUST, B), jnp.float32, jnp.log(0.5), jnp.log(3.0)))
    noise = jax.random.truncated_normal(keys[2], -4.0, 4.0, (NBLK * R, B), jnp.float32)
    padded = jnp.pad(noise, ((0, 0), (1, 1)))
    mixed = noise + 0.4 * (padded[:, 2:] + padded[:, :-2])
    values = means[labels] + spread[labels] * mixed
    return values.astype(jnp.bfloat16)


def steps_of(rng, extent, cuts, least, top_value):
    def one(dim, parts):
        draws = jax.random.uniform(jax.random.fold_in(jax.random.fold_in(rng, 6), dim), (parts,), jnp.float32, least / len(cuts), top_value / len(cuts))
        return jnp.repeat(jnp.exp(draws), extent[dim] // parts).reshape((-1,) + (1,) * (len(extent) - dim - 1))

    loudness = one(*cuts[0])
    for cut in cuts[1:]:
        loudness = loudness * one(*cut)
    return loudness


def scatter_about(stream_key, extent, scale, bound, pieces=(), kind=jnp.bfloat16):
    gain = steps_of(stream_key, extent, pieces, -0.22, 0.18) if pieces else 1.0
    array = jax.random.normal(stream_key, extent, jnp.float32) * scale * gain
    return jnp.minimum(jnp.maximum(array, -bound), bound).astype(kind)


def setup_inputs(seed: int = 0) -> dict:
    splits = jax.random.split(jax.random.key(seed), 4)
    pixels = draw_pixels(jax.random.fold_in(splits[3], 71), 0)
    labels = draw_labels(jax.random.fold_in(splits[3], 71), 0)
    targets = scatter_about(splits[2], (NT, B), 1.0, 6.0, ((0, 4),))
    return {"pixels": pixels, "labels": labels, "targets": targets}


def slot_numbers(lab_block):
    clusters = jnp.arange(NCLUST, dtype=jnp.int32)
    member = (lab_block[:, None] == clusters[None, :]).astype(jnp.int32)
    place_rank = jnp.sum(jnp.cumsum(member, axis=0) * member, axis=1) - 1
    return (lab_block * CAP + place_rank).astype(jnp.int32)

def group_block(pix_block, lab_block):
    slot_index = slot_numbers(lab_block)
    table = jnp.zeros((NCLUST * CAP, B), pix_block.dtype).at[slot_index].set(pix_block)
    return (table.reshape(NCLUST, CAP, B), slot_index)

def reference(pixels, labels, targets):
    block_count = pixels.shape[0] // R
    pix_blocks = pixels.reshape(block_count, R, B)
    lab_blocks = labels.reshape(block_count, R)

    def accumulate(running, block_item):
        grouped, slot_index = group_block(block_item[0], block_item[1])
        gram_part = jnp.einsum('cwb,cwd->cbd', grouped.astype(jnp.float32), grouped.astype(jnp.float32), preferred_element_type=jnp.float32)
        sum_part = jnp.sum(grouped, axis=1, dtype=jnp.float32)
        return ((running[0] + gram_part, running[1] + sum_part), None)
    start_state = (jnp.zeros((NCLUST, B, B), jnp.float32), jnp.zeros((NCLUST, B), jnp.float32))
    (gram_sum, first_sums), _ = lax.scan(accumulate, start_state, (pix_blocks, lab_blocks))
    clusters = jnp.arange(NCLUST, dtype=jnp.int32)
    counts = jnp.sum((labels[:, None] == clusters[None, :]).astype(jnp.float32), axis=0)
    counts = jnp.maximum(counts, 1.0)
    centre = first_sums / counts[:, None]
    identity = jnp.eye(B, dtype=jnp.float32)
    covariance = gram_sum / counts[:, None, None] - centre[:, :, None] * centre[:, None, :] + 0.05 * identity
    factor = jnp.linalg.cholesky(covariance)
    inverse = jax.scipy.linalg.solve_triangular(factor, jnp.broadcast_to(identity, factor.shape), lower=True)
    whitened = jnp.einsum('tb,cdb->ctd', targets.astype(jnp.float32), inverse, precision=lax.Precision.HIGHEST)
    lib_norm = jnp.sum(whitened * whitened, axis=-1)

    def score_block(block_item):
        grouped, slot_index = group_block(block_item[0], block_item[1])
        centered = grouped.astype(jnp.float32) - centre[:, None, :]
        white_pix = jnp.einsum('cwb,cdb->cwd', centered, inverse, precision=lax.Precision.HIGHEST)
        inner_prod = jnp.einsum('cwd,ctd->cwt', white_pix, whitened, precision=lax.Precision.HIGHEST)
        pix_norm = jnp.sum(white_pix * white_pix, axis=-1)
        result = B * inner_prod * inner_prod / ((lib_norm[:, None, :] + 1e-06) * (pix_norm[:, :, None] + 1e-06))
        result = result.astype(jnp.bfloat16).reshape(NCLUST * CAP, NT)
        return result[slot_index]
    scores = lax.map(score_block, (pix_blocks, lab_blocks))
    return scores.reshape(block_count * R, NT)
```

```python
import functools

import jax
import jax.numpy as jnp
from jax import lax
from jax.experimental import pallas as pl
from jax.experimental.pallas import tpu as pltpu
from jax.sharding import PartitionSpec as P

NCLUST = 64
CAP = 8
RIDGE = 0.05
EPS = 1e-06
STEP = 64
LANES = 128
SUB = 8
PIV = 4
OWNED = 2
MESH = pl.DeviceIdType.MESH
F32 = jnp.float32
BF16 = jnp.bfloat16


def dot_t(a, b):
    return lax.dot_general(a, b, (((1,), (1,)), ((), ())), preferred_element_type=F32)


def dot_0(a, b):
    return lax.dot_general(a, b, (((0,), (0,)), ((), ())), preferred_element_type=F32)


def dot_n(a, b):
    return lax.dot_general(a, b, (((1,), (0,)), ((), ())), preferred_element_type=F32)


def halves(v):
    big = v.astype(BF16)
    return big, (v - big.astype(F32)).astype(BF16)


def thirds(v):
    big, rest = v.astype(BF16), v
    rest = rest - big.astype(F32)
    mid = rest.astype(BF16)
    return big, mid, (rest - mid.astype(F32)).astype(BF16)


def six_left(t, axis):
    return jnp.concatenate([t[0], t[0], t[1], t[0], t[1], t[2]], axis=axis)


def six_right(t, axis):
    return jnp.concatenate([t[0], t[1], t[0], t[2], t[1], t[0]], axis=axis)


def pair_rows(t, c):
    zero = jnp.zeros_like(t)
    return jnp.concatenate([zero] * c + [t] + [zero] * (OWNED - 1 - c), axis=0)


def grow(v, rows, width):
    if v.shape[1] < width:
        v = jnp.concatenate([v, jnp.zeros((v.shape[0], width - v.shape[1]), v.dtype)], axis=1)
    if v.shape[0] < rows:
        v = jnp.concatenate([v, jnp.zeros((rows - v.shape[0], v.shape[1]), v.dtype)], axis=0)
    return v


def pivot_inverse(e):
    r = 1.0 / (e[0][0] * e[1][1] - e[0][1] * e[0][1])
    i00, i01, i11 = e[1][1] * r, -e[0][1] * r, e[0][0] * r
    x00 = i00 * e[0][2] + i01 * e[1][2]
    x01 = i00 * e[0][3] + i01 * e[1][3]
    x10 = i01 * e[0][2] + i11 * e[1][2]
    x11 = i01 * e[0][3] + i11 * e[1][3]
    s00 = e[2][2] - (e[0][2] * x00 + e[1][2] * x10)
    s01 = e[2][3] - (e[0][2] * x01 + e[1][2] * x11)
    s11 = e[3][3] - (e[0][3] * x01 + e[1][3] * x11)
    q = 1.0 / (s00 * s11 - s01 * s01)
    t00, t01, t11 = s11 * q, -s01 * q, s00 * q
    y00 = -(x00 * t00 + x01 * t01)
    y01 = -(x00 * t01 + x01 * t11)
    y10 = -(x10 * t00 + x11 * t01)
    y11 = -(x10 * t01 + x11 * t11)
    n00 = i00 - (y00 * x00 + y01 * x01)
    n01 = i01 - (y00 * x10 + y01 * x11)
    n11 = i11 - (y10 * x10 + y11 * x11)
    return [[n00, n01, y00, y01], [n01, n11, y10, y11], [y00, y10, t00, t01], [y01, y11, t01, t11]]


def paired_inverse(tile):
    rows = tile.shape[0]
    lanes = lax.broadcasted_iota(jnp.int32, (SUB, LANES), 1)
    sub = lax.broadcasted_iota(jnp.int32, (SUB, LANES), 0)
    base = jnp.where(lanes < STEP, 0, STEP)
    inside = lanes - base
    parts = [tile[g : g + SUB] for g in range(0, rows, SUB)]
    for j in range(0, rows, PIV):
        home, at = j // SUB, j % SUB
        cols = [[jnp.take_along_axis(p, base + (j + c), axis=1) for c in range(PIV)] for p in parts]
        spread = lambda v, a: jnp.broadcast_to(v[at + a : at + a + 1, :], (SUB, LANES))
        inv = pivot_inverse([[spread(cols[home][c], a) if a <= c else None for c in range(PIV)] for a in range(PIV)])
        block = (inside >= j) & (inside < j + PIV)
        src = [jnp.where(block, jnp.where(inside == j + c, 1.0, 0.0), spread(parts[home], c)) for c in range(PIV)]
        norm = [(inv[a][0] * src[0] + inv[a][1] * src[1]) + (inv[a][2] * src[2] + inv[a][3] * src[3]) for a in range(PIV)]
        fresh = []
        for g, p in enumerate(parts):
            col = cols[g]
            rest = jnp.where(block, 0.0, p) - (
                (col[0] * norm[0] + col[1] * norm[1]) + (col[2] * norm[2] + col[3] * norm[3])
            )
            if g == home:
                for a in range(PIV):
                    rest = jnp.where(sub == at + a, norm[a], rest)
            fresh.append(rest)
        parts = fresh
    return jnp.concatenate(parts, axis=0)


class Eliminate:
    def __init__(self):
        self.inverse = [None] * OWNED
        self.k = 0

    def add(self, rows):
        k = self.k
        wide = rows[0].shape[1]
        old = -(-k * STEP // LANES) * LANES
        lane = lax.broadcasted_iota(jnp.int32, (STEP, LANES), 1)
        own = [m[:, k * STEP // LANES * LANES :][:, :LANES] for m in rows]
        odd = k % 2
        own[1 - odd] = pltpu.roll(own[1 - odd], STEP, 1)
        pair = jnp.where(lane < STEP, own[0], own[1])
        lifts = []
        if k:
            lefts, rights = [], []
            for c, m in enumerate(rows):
                r3 = thirds(m[:, :old])
                lift = dot_n(six_left(r3, 1), six_right(thirds(self.inverse[c]), 0))
                lifts.append(lift)
                lefts.append(six_left(thirds(lift), 1))
                rights.append(six_right([pair_rows(t, c) for t in r3], 1))
            pair = pair - dot_t(jnp.concatenate(lefts, axis=1), jnp.concatenate(rights, axis=1))
        pair = paired_inverse(pair)
        wl = lax.broadcasted_iota(jnp.int32, (STEP, wide), 1)
        ws = lax.broadcasted_iota(jnp.int32, (STEP, wide), 0)
        eye = jnp.where(wl == ws + k * STEP, 1.0, 0.0)
        if not k:
            turned = pltpu.roll(pair, STEP, 1)
            self.inverse = [grow(jnp.where(lane < STEP, v, 0.0), LANES, LANES) for v in (pair, turned)]
        else:
            left = six_left(thirds(pair), 1)
            for c in range(OWNED):
                q3 = thirds(eye - grow(lifts[c], STEP, wide))
                w = dot_n(left, six_right([pair_rows(t, c) for t in q3], 0))
                upd = dot_0(six_left(q3, 0), six_right(thirds(w), 0))
                self.inverse[c] = grow(self.inverse[c], wide, wide) + upd
        self.k = k + 1


def slot_of(lab, me, devices):
    count = lab.shape[1]
    ri = lax.broadcasted_iota(jnp.int32, (count, count), 0)
    ci = lax.broadcasted_iota(jnp.int32, (count, count), 1)
    lab_row = lab.astype(F32)
    lab_col = jnp.sum(jnp.where(ri == ci, lab_row, 0.0), axis=1, keepdims=True)
    same = jnp.where(lab_row == lab_col, 1.0, 0.0)
    rank_col = jnp.sum(jnp.where(ci < ri, same, 0.0), axis=1, keepdims=True).astype(jnp.int32)
    rank_row = jnp.sum(jnp.where(ri < ci, same, 0.0), axis=0, keepdims=True).astype(jnp.int32)
    lab_col = lab_col.astype(jnp.int32)
    hop = lambda v: jnp.bitwise_xor(lax.shift_right_logical(v, 1), me)
    side = lambda v: jnp.bitwise_and(v, 1)
    slots = devices * CAP
    down = lax.broadcasted_iota(jnp.int32, (slots, count), 0)
    put = [
        jnp.where(down == jnp.where(side(lab) == c, hop(lab) * CAP + rank_row, -1), 1.0, 0.0).astype(BF16)
        for c in range(OWNED)
    ]
    across = lax.broadcasted_iota(jnp.int32, (count, slots * OWNED), 1)
    take = jnp.where(across == (hop(lab_col) * OWNED + side(lab_col)) * CAP + rank_col, 1.0, 0.0).astype(BF16)
    far = lax.broadcasted_iota(jnp.int32, (devices, count), 0)
    lane = lax.broadcasted_iota(jnp.int32, (count, LANES), 1)
    near = jnp.where(lax.div(lane, STEP) == side(lab_col), 1.0, 0.0).astype(BF16)
    tally = dot_n(jnp.where(far == hop(lab), 1.0, 0.0).astype(BF16), near)
    return take, put, tally


def step_body(
    bands, n_tile, n_grp,
    lab_ref, pix_ref, tgt_ref, out_ref,
    outgoing, arrived, counts, heard, library, outbound, returned, take_ref,
    send_n, recv_n, send_a, recv_a, send_t, recv_t, send_b, recv_b,
):
    devices = n_tile * n_grp
    full, rest = bands // LANES, bands % LANES
    flag = OWNED * rest
    total = outbound.shape[2]
    size = devices * CAP
    blocks = size // STEP
    span = STEP // CAP
    tile = lax.axis_index("tile")
    grp = lax.axis_index("grp")
    me = tile * n_grp + grp

    def flip(v, r):
        out = v
        for k in range(r.bit_length()):
            if (r >> k) & 1:
                out = out + (1 - 2 * lax.rem(lax.div(v, 1 << k), 2)) * (1 << k)
        return out

    def place(r):
        return (flip(tile, r // n_grp), flip(grp, r % n_grp))

    barrier = pltpu.get_barrier_semaphore()
    for r in range(devices - 1, 0, -1):
        pl.semaphore_signal(barrier, inc=1, device_id=place(r), device_id_type=MESH)

    take, put, tally = slot_of(lab_ref[...], me, devices)
    take_ref[...] = take
    counts[...] = tally.reshape(devices, 1, LANES)
    heard[0] = counts[0]
    for c in range(OWNED):
        body = dot_t(put[c], pix_ref[: full * LANES, :])
        for t in range(full):
            at = (c * full + t) * SUB
            outgoing[:, at : at + SUB, :] = body[:, t * LANES : (t + 1) * LANES].astype(BF16).reshape(devices, SUB, LANES)
    tail = pix_ref[full * LANES :, :]
    pad = LANES - flag
    mark = lax.broadcasted_iota(jnp.int32, (pad, tail.shape[1]), 0)
    ends = [
        jnp.concatenate(
            [tail if i == c else jnp.zeros_like(tail) for i in range(OWNED)]
            + [jnp.where(mark == c, 1.0, 0.0).astype(BF16)],
            axis=0,
        )
        for c in range(OWNED)
    ]
    ends = dot_t(jnp.concatenate(put, axis=1), jnp.concatenate(ends, axis=1))
    outgoing[:, OWNED * full * SUB :, :] = ends.astype(BF16).reshape(devices, SUB, LANES)
    arrived[0] = outgoing[0]
    library[grp] = tgt_ref[...]
    pl.semaphore_wait(barrier, devices - 1)

    def ship(src, dst, sends, recvs, r):
        return pltpu.make_async_remote_copy(
            src_ref=src.at[r], dst_ref=dst.at[r],
            send_sem=sends.at[r], recv_sem=recvs.at[r],
            device_id=place(r), device_id_type=MESH,
        )

    tell = lambda r: ship(counts, heard, send_n, recv_n, r)
    go = lambda r: ship(outgoing, arrived, send_a, recv_a, r)
    back = lambda r: ship(outbound, returned, send_b, recv_b, r)

    def lend(i, src, home, to):
        return pltpu.make_async_remote_copy(
            src_ref=src, dst_ref=library.at[home], send_sem=send_t.at[i], recv_sem=recv_t.at[i],
            device_id=(tile, flip(grp, to)), device_id_type=MESH,
        )

    across = flip(grp, 2)
    lends = [lend(0, tgt_ref, grp, 1), lend(1, tgt_ref, grp, 2), lend(2, library.at[across], across, 1)]
    half = devices // 2
    for r in range(devices - 1, 0, -1):
        tell(r).start()
    for r in range(half):
        go(half + r).start()
        if r:
            go(r).start()
    lends[0].start()
    lends[1].start()

    lane = lax.broadcasted_iota(jnp.int32, (STEP, LANES), 1)
    own = [((lane >= c * rest) & (lane < (c + 1) * rest)) for c in range(OWNED)]
    kept = [own[c] | (lane == flag + c) for c in range(OWNED)]
    sign = lax.broadcasted_iota(jnp.int32, (16, (full + 1) * LANES), 1)
    sign = [jnp.where(sign == full * LANES + flag + c, 1.0, 0.0).astype(BF16) for c in range(OWNED)]
    lefts = [[] for _ in range(OWNED)]
    rights = [[] for _ in range(OWNED)]
    valid = [[] for _ in range(OWNED)]
    centre = [None] * OWNED
    state = Eliminate()
    number = None
    held = {}

    def load(b):
        arr = arrived[b * span : (b + 1) * span].astype(F32)
        cut = lambda i: arr[:, i * SUB : (i + 1) * SUB, :].reshape(STEP, LANES)
        edge = cut(OWNED * full)
        out = []
        for c in range(OWNED):
            main = [cut(c * full + t) for t in range(full)]
            x = jnp.concatenate(main + [edge], axis=1)
            if b == 0:
                tops = jnp.maximum(jnp.sum(edge[:, flag + c : flag + c + 1]), 1.0)
                mid = jnp.concatenate(main + [jnp.where(own[c], edge, 0.0)], axis=1)
                mid = jnp.sum(mid, axis=0, keepdims=True) * (1.0 / tops)
                mid = mid.astype(BF16)
                centre[c] = (mid, mid.astype(F32))
            lefts[c].append(x.astype(BF16))
            rights[c].append(jnp.concatenate(main + [jnp.where(kept[c], edge, 0.0)], axis=1).astype(BF16))
            valid[c].append(edge[:, flag + c : flag + c + 1])
            out.append(jnp.sum(x * centre[c][1], axis=1, keepdims=True))
        return out

    def gram(b, lean):
        rows = []
        wide = -(-(b + 1) * STEP // LANES) * LANES
        for c in range(OWNED):
            mid, midf = centre[c]
            left = jnp.concatenate([lefts[c][b], jnp.broadcast_to(mid, (16, mid.shape[1])), sign[c]], axis=0)
            right = jnp.concatenate(rights[c], axis=0)
            if right.shape[0] < wide:
                right = jnp.concatenate([right, jnp.zeros((wide - right.shape[0], right.shape[1]), BF16)], axis=0)
            g = dot_t(left, right)
            along, has = g[STEP : STEP + 1], g[STEP + 16 : STEP + 17]
            along = along - jnp.sum(midf * midf) * has
            rows.append(g[:STEP] - valid[c][b] * along - lean[c] * has)
        return rows

    def scale(b, rows):
        wide = rows[0].shape[1]
        wl = lax.broadcasted_iota(jnp.int32, (STEP, wide), 1)
        ws = lax.broadcasted_iota(jnp.int32, (STEP, wide), 0)
        diag = wl == ws + b * STEP
        return [m + jnp.where(diag, number[c] * RIDGE, 0.0) for c, m in enumerate(rows)]

    for b in range(blocks):
        for r in range(b * span, (b + 1) * span):
            if r:
                go(r).wait_recv()
        rows = gram(b, load(b))
        if b == 0:
            for r in range(1, devices):
                tell(r).wait_recv()
            heads = jnp.maximum(jnp.sum(heard[...], axis=0), 1.0)
            number = [heads[:, c * STEP : c * STEP + 1] for c in range(OWNED)]
        if b == 1:
            lends[1].wait_recv()
            lends[2].start()
        if b == blocks - 1:
            for i in (0, 2):
                lends[i].wait_recv()
            targets = jnp.concatenate([library[i] for i in range(n_grp)], axis=1)
            tf = targets.astype(F32)
            held["norm"] = jnp.sum(tf * tf, axis=0, keepdims=True)
            zero = jnp.zeros((rest, total), BF16)
            for c in range(OWNED):
                lib = [targets[: full * LANES]]
                lib += [targets[full * LANES :] if i == c else zero for i in range(OWNED)]
                lib += [jnp.zeros((pad, total), BF16)]
                u = dot_n(jnp.concatenate(lefts[c], axis=0), jnp.concatenate(lib, axis=0))
                v = jnp.concatenate(valid[c], axis=0)
                held[c] = (u - jnp.sum(u, axis=0, keepdims=True) * (1.0 / number[c])) * v
        state.add(scale(b, rows))

    diag = lax.broadcasted_iota(jnp.int32, (LANES, LANES), 0) == lax.broadcasted_iota(jnp.int32, (LANES, LANES), 1)
    res = []
    for c in range(OWNED):
        inv, u, n = state.inverse[c], held[c], number[c]
        i1, i2, i3 = thirds(inv)
        u1, u2 = halves(u)
        z = dot_n(jnp.concatenate([i1, i1, i2], axis=1), jnp.concatenate([u1, u2, u1], axis=0))
        v = jnp.broadcast_to(jnp.concatenate(valid[c], axis=0), (size, LANES)).astype(BF16)
        p = dot_n(jnp.concatenate([i1, i2, i3], axis=1), jnp.concatenate([v, v, v], axis=0))
        s = jnp.sum(p, axis=0, keepdims=True)
        s = jnp.where(s > 0.0, 1.0 / jnp.where(s > 0.0, s, 1.0), 0.0)
        w = jnp.sum(z, axis=0, keepdims=True)
        ws = w * s[:, 0:1]
        lib = (held["norm"] - jnp.sum(u * z, axis=0, keepdims=True) + w * ws) * (1.0 / RIDGE)
        lib = jnp.maximum(lib, 0.0) + EPS
        kd = jnp.concatenate(
            [
                jnp.sum(jnp.where(diag, inv[i : i + LANES, i : i + LANES], 0.0), axis=1, keepdims=True)
                for i in range(0, size, LANES)
            ],
            axis=0,
        )
        kd = kd - p * p * s
        pix = n * (1.0 - (n * RIDGE) * kd) - 1.0
        pix = jnp.maximum(pix, 0.0) + EPS
        gain = (n * n * bands) / pix
        lib = 1.0 / lib
        pieces = []
        for i in range(0, total, LANES):
            d = z[:, i : i + LANES] - p * ws[:, i : i + LANES]
            pieces.append(d * d * gain * lib[:, i : i + LANES])
        res.append(jnp.concatenate(pieces, axis=1).reshape(devices, 1, CAP, total))
    joined = jnp.concatenate(res, axis=1).reshape(devices, OWNED * CAP, total).astype(BF16)
    for lo, hi in ((half, devices), (0, half)):
        outbound[lo:hi] = joined[lo:hi]
        for r in range(hi - 1, max(lo, 1) - 1, -1):
            back(r).start()
    returned[0] = outbound[0]
    for r in range(1, devices):
        tell(r).wait_send()
        go(r).wait_send()
    for cp in lends:
        cp.wait_send()
    for r in range(1, devices):
        back(r).wait()
    out_ref[...] = dot_n(take_ref[...], returned[...].reshape(size * OWNED, total)).astype(BF16)


def narrow(pixels, labels, targets):
    n_tile, n_grp = lax.axis_size("tile"), lax.axis_size("grp")
    devices = n_tile * n_grp
    rows, bands = pixels.shape
    total = targets.shape[0] * n_grp
    deep = (OWNED * (bands // LANES) + 1) * SUB
    vmem = pl.BlockSpec(memory_space=pltpu.VMEM)
    dma = pltpu.SemaphoreType.DMA
    return pl.pallas_call(
        functools.partial(step_body, bands, n_tile, n_grp),
        out_shape=jax.ShapeDtypeStruct((rows, total), BF16),
        in_specs=[vmem] * 3,
        out_specs=vmem,
        scratch_shapes=[
            pltpu.VMEM((devices, deep, LANES), BF16),
            pltpu.VMEM((devices, deep, LANES), BF16),
            pltpu.VMEM((devices, 1, LANES), F32),
            pltpu.VMEM((devices, 1, LANES), F32),
            pltpu.VMEM((n_grp, bands, targets.shape[0]), BF16),
            pltpu.VMEM((devices, OWNED * CAP, total), BF16),
            pltpu.VMEM((devices, OWNED * CAP, total), BF16),
            pltpu.VMEM((rows, NCLUST * CAP), BF16),
            dma((devices,)), dma((devices,)),
            dma((devices,)), dma((devices,)),
            dma((n_grp,)), dma((n_grp,)),
            dma((devices,)), dma((devices,)),
        ],
        compiler_params=pltpu.CompilerParams(
            collective_id=0, has_side_effects=True, vmem_limit_bytes=60 * 1024 * 1024
        ),
    )(labels.reshape(1, rows), pixels.T, targets.T)


def wide_cluster(pixels, labels, targets):
    n_tile = lax.axis_size("tile")
    n_grp = lax.axis_size("grp")
    band_count = pixels.shape[1]
    per_owner = 2 * NCLUST // n_tile
    target_total = targets.shape[0] * n_grp
    clusters = jnp.arange(NCLUST, dtype=jnp.int32)
    member = (labels[:, None] == clusters[None, :]).astype(jnp.int32)
    local_count = jnp.sum(member, axis=0).astype(jnp.float32)
    counts = lax.psum(local_count, ("tile", "grp"))
    place_rank = jnp.sum(jnp.cumsum(member, axis=0) * member, axis=1) - 1
    owner_pair = labels // per_owner
    inner_slot = labels % per_owner
    slot_width = CAP
    target_tile = 2 * owner_pair
    slot_index = (target_tile * per_owner + inner_slot) * slot_width + place_rank
    slot_total = n_tile * per_owner * slot_width
    outgoing = jnp.zeros((slot_total, band_count), jnp.bfloat16).at[slot_index].set(pixels)
    outgoing = outgoing.reshape(n_tile, per_owner * slot_width, band_count)
    arrived = lax.all_to_all(outgoing, "tile", split_axis=0, concat_axis=0, tiled=True)
    grouped = arrived.reshape(n_tile, per_owner, slot_width, band_count)
    gram_sum = jnp.einsum("scwb,scwd->cbd", grouped, grouped, preferred_element_type=jnp.float32)
    first_sums = jnp.sum(grouped, axis=(0, 2), dtype=jnp.float32)
    gram_sum, first_sums = lax.psum((gram_sum, first_sums), "grp")
    own_pair = lax.axis_index("tile") // 2
    own_counts = lax.dynamic_slice_in_dim(counts, own_pair * per_owner, per_owner, 0)
    own_counts = jnp.maximum(own_counts, 1.0)
    centre = first_sums / own_counts[:, None]
    identity = jnp.eye(band_count, dtype=jnp.float32)
    covariance = (
        gram_sum / own_counts[:, None, None]
        - centre[:, :, None] * centre[:, None, :]
        + 0.05 * identity
    )
    factor = jnp.linalg.cholesky(covariance)
    inverse = jax.scipy.linalg.solve_triangular(
        factor, jnp.broadcast_to(identity, factor.shape), lower=True
    )
    whitened = jnp.einsum(
        "tb,cdb->ctd",
        lax.all_gather(targets, "grp", axis=0, tiled=True).astype(jnp.float32),
        inverse,
        precision=lax.Precision.HIGHEST,
    )
    lib_norm = jnp.sum(whitened * whitened, axis=-1)
    centered = grouped.astype(jnp.float32) - centre[None, :, None, :]
    white_pix = jnp.einsum("scwb,cdb->scwd", centered, inverse, precision=lax.Precision.HIGHEST)
    inner_prod = jnp.einsum("scwd,ctd->scwt", white_pix, whitened, precision=lax.Precision.HIGHEST)
    pix_norm = jnp.sum(white_pix * white_pix, axis=-1)
    result = (
        band_count
        * inner_prod
        * inner_prod
        / ((lib_norm[None, :, None, :] + 1e-06) * (pix_norm[:, :, :, None] + 1e-06))
    )
    outbound = result.astype(jnp.bfloat16).reshape(n_tile, per_owner * slot_width, target_total)
    returned = lax.all_to_all(outbound, "tile", split_axis=0, concat_axis=0, tiled=True)
    flat_scores = returned.reshape(slot_total, target_total)
    return flat_scores[slot_index]


def local(pixels, labels, targets):
    n_tile, n_grp = lax.axis_size("tile"), lax.axis_size("grp")
    devices = n_tile * n_grp
    rest = pixels.shape[1] % LANES
    if (
        NCLUST == OWNED * devices
        and n_grp == 4
        and n_tile & (n_tile - 1) == 0
        and devices * CAP % (2 * STEP) == 0
        and rest % 16 == 0
        and OWNED * (rest + 1) <= LANES
    ):
        return narrow(pixels, labels, targets)
    return wide_cluster(pixels, labels, targets)


def solution(mesh):
    return jax.shard_map(
        local,
        mesh=mesh,
        in_specs=(P(("tile", "grp"), None), P(("tile", "grp")), P("grp", None)),
        out_specs=P(("tile", "grp"), None),
        check_vma=False,
    )
```

```python
import functools

import jax
import jax.numpy as jnp
from jax import lax
from jax.experimental import pallas as pl
from jax.experimental.pallas import tpu as pltpu
from jax.sharding import PartitionSpec as P

NCLUST = 64
CAP = 8
RIDGE = 0.05
EPS = 1e-06
STEP = 64
LANES = 128
SUB = 8
PIV = 4
OWNED = 2
MESH = pl.DeviceIdType.MESH
F32 = jnp.float32
BF16 = jnp.bfloat16


def dot_t(a, b):
    return lax.dot_general(a, b, (((1,), (1,)), ((), ())), preferred_element_type=F32)


def dot_0(a, b):
    return lax.dot_general(a, b, (((0,), (0,)), ((), ())), preferred_element_type=F32)


def dot_n(a, b):
    return lax.dot_general(a, b, (((1,), (0,)), ((), ())), preferred_element_type=F32)


def halves(v):
    big = v.astype(BF16)
    return big, (v - big.astype(F32)).astype(BF16)


def thirds(v):
    big, rest = v.astype(BF16), v
    rest = rest - big.astype(F32)
    mid = rest.astype(BF16)
    return big, mid, (rest - mid.astype(F32)).astype(BF16)


def six_left(t, axis):
    return jnp.concatenate([t[0], t[0], t[1], t[0], t[1], t[2]], axis=axis)


def six_right(t, axis):
    return jnp.concatenate([t[0], t[1], t[0], t[2], t[1], t[0]], axis=axis)


def pair_rows(t, c):
    zero = jnp.zeros_like(t)
    return jnp.concatenate([zero] * c + [t] + [zero] * (OWNED - 1 - c), axis=0)


def grow(v, rows, width):
    if v.shape[1] < width:
        v = jnp.concatenate([v, jnp.zeros((v.shape[0], width - v.shape[1]), v.dtype)], axis=1)
    if v.shape[0] < rows:
        v = jnp.concatenate([v, jnp.zeros((rows - v.shape[0], v.shape[1]), v.dtype)], axis=0)
    return v


def pivot_inverse(e):
    r = 1.0 / (e[0][0] * e[1][1] - e[0][1] * e[0][1])
    i00, i01, i11 = e[1][1] * r, -e[0][1] * r, e[0][0] * r
    x00 = i00 * e[0][2] + i01 * e[1][2]
    x01 = i00 * e[0][3] + i01 * e[1][3]
    x10 = i01 * e[0][2] + i11 * e[1][2]
    x11 = i01 * e[0][3] + i11 * e[1][3]
    s00 = e[2][2] - (e[0][2] * x00 + e[1][2] * x10)
    s01 = e[2][3] - (e[0][2] * x01 + e[1][2] * x11)
    s11 = e[3][3] - (e[0][3] * x01 + e[1][3] * x11)
    q = 1.0 / (s00 * s11 - s01 * s01)
    t00, t01, t11 = s11 * q, -s01 * q, s00 * q
    y00 = -(x00 * t00 + x01 * t01)
    y01 = -(x00 * t01 + x01 * t11)
    y10 = -(x10 * t00 + x11 * t01)
    y11 = -(x10 * t01 + x11 * t11)
    n00 = i00 - (y00 * x00 + y01 * x01)
    n01 = i01 - (y00 * x10 + y01 * x11)
    n11 = i11 - (y10 * x10 + y11 * x11)
    return [[n00, n01, y00, y01], [n01, n11, y10, y11], [y00, y10, t00, t01], [y01, y11, t01, t11]]


def paired_factor(tile, fill):
    rows = tile.shape[0]
    lanes = lax.broadcasted_iota(jnp.int32, (SUB, LANES), 1)
    sub = lax.broadcasted_iota(jnp.int32, (SUB, LANES), 0)
    base = jnp.where(lanes < STEP, 0, STEP)
    inside = lanes - base
    parts = [tile[g : g + SUB] for g in range(0, rows, SUB)]
    low, scaled = [], []
    for j in range(0, rows, PIV):
        home, at = j // SUB, j % SUB
        pick = lambda p: [jnp.take_along_axis(p, base + (j + c), axis=1) for c in range(PIV)]
        spread = lambda v, a: jnp.broadcast_to(v[at + a : at + a + 1, :], (SUB, LANES))
        first = pick(parts[home])
        inv = pivot_inverse([[spread(first[c], a) if a <= c else None for c in range(PIV)] for a in range(PIV)])
        block = (inside >= j) & (inside < j + PIV)
        src = [jnp.where(block, jnp.where(inside == j + c, 1.0, 0.0), spread(parts[home], c)) for c in range(PIV)]
        norm = [(inv[a][0] * src[0] + inv[a][1] * src[1]) + (inv[a][2] * src[2] + inv[a][3] * src[3]) for a in range(PIV)]
        if not at:
            low.append(jnp.zeros((SUB, LANES), F32))
            scaled.append(jnp.zeros((SUB, LANES), F32))
        done = inside < j + PIV
        for a in range(PIV):
            here = (sub == at + a) & done
            low[home] = jnp.where(here, src[a], low[home])
            scaled[home] = jnp.where(here, norm[a], scaled[home])
        for g in range(home if at + PIV < SUB else home + 1, rows // SUB):
            col = first if g == home else pick(parts[g])
            parts[g] = jnp.where(block, 0.0, parts[g]) - (
                (col[0] * norm[0] + col[1] * norm[1]) + (col[2] * norm[2] + col[3] * norm[3])
            )
        if fill:
            fill.pop(0)()
    while fill:
        fill.pop(0)()
    return jnp.concatenate(low + scaled, axis=0)


class Eliminate:
    def __init__(self):
        self.inverse = [None] * OWNED
        self.k = 0

    def reduce(self, rows):
        k = self.k
        wide = rows[0].shape[1]
        old = -(-k * STEP // LANES) * LANES
        lane = lax.broadcasted_iota(jnp.int32, (STEP, LANES), 1)
        own = [m[:, k * STEP // LANES * LANES :][:, :LANES] for m in rows]
        odd = k % 2
        own[1 - odd] = pltpu.roll(own[1 - odd], STEP, 1)
        pair = jnp.where(lane < STEP, own[0], own[1])
        wl = lax.broadcasted_iota(jnp.int32, (STEP, wide), 1)
        ws = lax.broadcasted_iota(jnp.int32, (STEP, wide), 0)
        eye = jnp.where(wl == ws + k * STEP, 1.0, 0.0)
        if not k:
            return pair, [eye] * OWNED
        lefts, rights, maps = [], [], []
        for c, m in enumerate(rows):
            r3 = thirds(m[:, :old])
            lift = dot_n(six_left(r3, 1), six_right(thirds(self.inverse[c]), 0))
            maps.append(eye - grow(lift, STEP, wide))
            lefts.append(six_left(thirds(lift), 1))
            rights.append(six_right([pair_rows(t, c) for t in r3], 1))
        return pair - dot_t(jnp.concatenate(lefts, axis=1), jnp.concatenate(rights, axis=1)), maps

    def extend(self, factor, maps):
        wide = maps[0].shape[1]
        lane = lax.broadcasted_iota(jnp.int32, factor.shape, 1)
        left = None if not self.k else six_left(thirds(factor), 1)
        for c in range(OWNED):
            if not self.k:
                both = factor if not c else pltpu.roll(factor, STEP, 1)
                both = jnp.where(lane < STEP, both, 0.0)
            else:
                q3 = thirds(maps[c])
                both = dot_n(left, six_right([pair_rows(t, c) for t in q3], 0))
            upd = dot_0(six_left(thirds(both[:STEP]), 0), six_right(thirds(both[STEP:]), 0))
            self.inverse[c] = upd if not self.k else grow(self.inverse[c], wide, wide) + upd
        self.k += 1


def slot_of(lab, me, devices):
    count = lab.shape[1]
    ri = lax.broadcasted_iota(jnp.int32, (count, count), 0)
    ci = lax.broadcasted_iota(jnp.int32, (count, count), 1)
    lab_row = lab.astype(F32)
    lab_col = jnp.sum(jnp.where(ri == ci, lab_row, 0.0), axis=1, keepdims=True)
    same = jnp.where(lab_row == lab_col, 1.0, 0.0)
    rank_col = jnp.sum(jnp.where(ci < ri, same, 0.0), axis=1, keepdims=True).astype(jnp.int32)
    rank_row = jnp.sum(jnp.where(ri < ci, same, 0.0), axis=0, keepdims=True).astype(jnp.int32)
    lab_col = lab_col.astype(jnp.int32)
    hop = lambda v: jnp.bitwise_xor(lax.shift_right_logical(v, 1), me)
    side = lambda v: jnp.bitwise_and(v, 1)
    slots = devices * CAP
    down = lax.broadcasted_iota(jnp.int32, (slots, count), 0)
    put = [
        jnp.where(down == jnp.where(side(lab) == c, hop(lab) * CAP + rank_row, -1), 1.0, 0.0).astype(BF16)
        for c in range(OWNED)
    ]
    across = lax.broadcasted_iota(jnp.int32, (count, slots * OWNED), 1)
    take = jnp.where(across == (hop(lab_col) * OWNED + side(lab_col)) * CAP + rank_col, 1.0, 0.0).astype(BF16)
    far = lax.broadcasted_iota(jnp.int32, (devices, count), 0)
    lane = lax.broadcasted_iota(jnp.int32, (count, LANES), 1)
    near = jnp.where(lax.div(lane, STEP) == side(lab_col), 1.0, 0.0).astype(BF16)
    tally = dot_n(jnp.where(far == hop(lab), 1.0, 0.0).astype(BF16), near)
    return take, put, tally


def step_body(
    bands, n_tile, n_grp,
    lab_ref, pix_ref, tgt_ref, out_ref,
    outgoing, arrived, counts, heard, library, outbound, returned, take_ref,
    send_n, recv_n, send_a, recv_a, send_t, recv_t, send_b, recv_b,
):
    devices = n_tile * n_grp
    full, rest = bands // LANES, bands % LANES
    flag = OWNED * rest
    total = outbound.shape[2]
    size = devices * CAP
    blocks = size // STEP
    span = STEP // CAP
    tile = lax.axis_index("tile")
    grp = lax.axis_index("grp")
    me = tile * n_grp + grp

    def flip(v, r):
        out = v
        for k in range(r.bit_length()):
            if (r >> k) & 1:
                out = out + (1 - 2 * lax.rem(lax.div(v, 1 << k), 2)) * (1 << k)
        return out

    def place(r):
        return (flip(tile, r // n_grp), flip(grp, r % n_grp))

    barrier = pltpu.get_barrier_semaphore()
    for r in range(devices - 1, 0, -1):
        pl.semaphore_signal(barrier, inc=1, device_id=place(r), device_id_type=MESH)

    take, put, tally = slot_of(lab_ref[...], me, devices)
    take_ref[...] = take
    counts[...] = tally.reshape(devices, 1, LANES)
    heard[0] = counts[0]
    for c in range(OWNED):
        body = dot_t(put[c], pix_ref[: full * LANES, :])
        for t in range(full):
            at = (c * full + t) * SUB
            outgoing[:, at : at + SUB, :] = body[:, t * LANES : (t + 1) * LANES].astype(BF16).reshape(devices, SUB, LANES)
    tail = pix_ref[full * LANES :, :]
    pad = LANES - flag
    mark = lax.broadcasted_iota(jnp.int32, (pad, tail.shape[1]), 0)
    ends = [
        jnp.concatenate(
            [tail if i == c else jnp.zeros_like(tail) for i in range(OWNED)]
            + [jnp.where(mark == c, 1.0, 0.0).astype(BF16)],
            axis=0,
        )
        for c in range(OWNED)
    ]
    ends = dot_t(jnp.concatenate(put, axis=1), jnp.concatenate(ends, axis=1))
    outgoing[:, OWNED * full * SUB :, :] = ends.astype(BF16).reshape(devices, SUB, LANES)
    arrived[0] = outgoing[0]
    library[grp] = tgt_ref[...]
    pl.semaphore_wait(barrier, devices - 1)

    def ship(src, dst, sends, recvs, r):
        return pltpu.make_async_remote_copy(
            src_ref=src.at[r], dst_ref=dst.at[r],
            send_sem=sends.at[r], recv_sem=recvs.at[r],
            device_id=place(r), device_id_type=MESH,
        )

    tell = lambda r: ship(counts, heard, send_n, recv_n, r)
    go = lambda r: ship(outgoing, arrived, send_a, recv_a, r)
    back = lambda r: ship(outbound, returned, send_b, recv_b, r)

    def lend(i, src, home, to):
        return pltpu.make_async_remote_copy(
            src_ref=src, dst_ref=library.at[home], send_sem=send_t.at[i], recv_sem=recv_t.at[i],
            device_id=(tile, flip(grp, to)), device_id_type=MESH,
        )

    across = flip(grp, 2)
    lends = [lend(0, tgt_ref, grp, 1), lend(1, tgt_ref, grp, 2), lend(2, library.at[across], across, 1)]
    half = devices // 2
    late = devices - span
    for r in range(devices - 1, 0, -1):
        tell(r).start()
    for r in range(1, half):
        go(r).start()
    for r in range(half, late):
        go(r).start()
    lends[0].start()
    lends[1].start()

    lane = lax.broadcasted_iota(jnp.int32, (STEP, LANES), 1)
    own = [((lane >= c * rest) & (lane < (c + 1) * rest)) for c in range(OWNED)]
    kept = [own[c] | (lane == flag + c) for c in range(OWNED)]
    sign = lax.broadcasted_iota(jnp.int32, (16, (full + 1) * LANES), 1)
    sign = [jnp.where(sign == full * LANES + flag + c, 1.0, 0.0).astype(BF16) for c in range(OWNED)]
    lefts = [[] for _ in range(OWNED)]
    rights = [[] for _ in range(OWNED)]
    valid = [[] for _ in range(OWNED)]
    centre = [None] * OWNED
    state = Eliminate()
    number = None
    held = {}

    def load(b):
        arr = arrived[b * span : (b + 1) * span].astype(F32)
        cut = lambda i: arr[:, i * SUB : (i + 1) * SUB, :].reshape(STEP, LANES)
        edge = cut(OWNED * full)
        out = []
        for c in range(OWNED):
            main = [cut(c * full + t) for t in range(full)]
            x = jnp.concatenate(main + [edge], axis=1)
            if b == 0:
                tops = jnp.maximum(jnp.sum(edge[:, flag + c : flag + c + 1]), 1.0)
                mid = jnp.concatenate(main + [jnp.where(own[c], edge, 0.0)], axis=1)
                mid = jnp.sum(mid, axis=0, keepdims=True) * (1.0 / tops)
                mid = mid.astype(BF16)
                centre[c] = (mid, mid.astype(F32))
            lefts[c].append(x.astype(BF16))
            rights[c].append(jnp.concatenate(main + [jnp.where(kept[c], edge, 0.0)], axis=1).astype(BF16))
            valid[c].append(edge[:, flag + c : flag + c + 1])
            out.append(jnp.sum(x * centre[c][1], axis=1, keepdims=True))
        return out

    def gram(b, lean):
        rows = []
        wide = -(-(b + 1) * STEP // LANES) * LANES
        for c in range(OWNED):
            mid, midf = centre[c]
            left = jnp.concatenate([lefts[c][b], jnp.broadcast_to(mid, (16, mid.shape[1])), sign[c]], axis=0)
            right = jnp.concatenate(rights[c], axis=0)
            if right.shape[0] < wide:
                right = jnp.concatenate([right, jnp.zeros((wide - right.shape[0], right.shape[1]), BF16)], axis=0)
            g = dot_t(left, right)
            along, has = g[STEP : STEP + 1], g[STEP + 16 : STEP + 17]
            along = along - jnp.sum(midf * midf) * has
            rows.append(g[:STEP] - valid[c][b] * along - lean[c] * has)
        return rows

    def scale(b, rows):
        wide = rows[0].shape[1]
        wl = lax.broadcasted_iota(jnp.int32, (STEP, wide), 1)
        ws = lax.broadcasted_iota(jnp.int32, (STEP, wide), 0)
        diag = wl == ws + b * STEP
        return [m + jnp.where(diag, number[c] * RIDGE, 0.0) for c, m in enumerate(rows)]

    def fetch(b):
        for r in range(max(b * span, 1), (b + 1) * span):
            go(r).wait_recv()
        return load(b)

    def measure(c):
        def run():
            lib = [held["lib"][: full * LANES]]
            lib += [held["lib"][full * LANES :] if i == c else jnp.zeros((rest, total), BF16) for i in range(OWNED)]
            lib += [jnp.zeros((pad, total), BF16)]
            u = dot_n(jnp.concatenate(lefts[c], axis=0), jnp.concatenate(lib, axis=0))
            v = jnp.concatenate(valid[c], axis=0)
            u = (u - jnp.sum(u, axis=0, keepdims=True) * (1.0 / number[c])) * v
            held[c] = jnp.concatenate([u, jnp.broadcast_to(v, (size, LANES))], axis=1)

        return run

    def advance(c):
        def run():
            u1, u2 = halves(held[c])
            m1, m2 = halves(jnp.concatenate([state.inverse[c][: size - STEP], held["maps"][c]], axis=0))
            z = dot_n(jnp.concatenate([m1, m1, m2], axis=1), jnp.concatenate([u1, u2, u1], axis=0))
            held["z", c] = z[: size - STEP]
            held["q", c] = z[size - STEP :]

        return run

    def summarise(c):
        def run():
            z = held["z", c]
            held["lib", c] = jnp.sum(held[c][: size - STEP] * z, axis=0, keepdims=True)
            held["sum", c] = jnp.sum(z, axis=0, keepdims=True)
            inv = state.inverse[c]
            held["diag", c] = [
                jnp.sum(jnp.where(diag, inv[i : i + LANES, i : i + LANES], 0.0), axis=1, keepdims=True)
                for i in range(0, size, LANES)
            ]

        return run

    def squares():
        tf = held["lib"].astype(F32)
        held["norm"] = jnp.sum(tf * tf, axis=0, keepdims=True)

    diag = lax.broadcasted_iota(jnp.int32, (LANES, LANES), 0) == lax.broadcasted_iota(jnp.int32, (LANES, LANES), 1)
    rows = gram(0, fetch(0))
    for r in range(1, devices):
        tell(r).wait_recv()
    heads = jnp.maximum(jnp.sum(heard[...], axis=0), 1.0)
    number = [heads[:, c * STEP : c * STEP + 1] for c in range(OWNED)]
    for r in range(late, devices):
        go(r).start()
    for b in range(blocks):
        pair, maps = state.reduce(scale(b, rows))
        if b < blocks - 1:
            factor = paired_factor(pair, [])
            state.extend(factor, maps)
            lean = fetch(b + 1)
            rows = gram(b + 1, lean)
            if not b:
                lends[1].wait_recv()
                lends[2].start()
    held["maps"] = maps
    for i in (0, 2):
        lends[i].wait_recv()
    held["lib"] = jnp.concatenate([library[i] for i in range(n_grp)], axis=1)
    state.inverse = [grow(m, size, size) for m in state.inverse]
    fill = [measure(0), measure(1), squares, advance(0), advance(1), summarise(0), summarise(1)]
    factor = paired_factor(pair, fill)

    f1, f2 = halves(factor)
    left = jnp.concatenate([f1, f1, f2], axis=1)
    res = []
    for c in range(OWNED):
        n = number[c]
        m1, m2 = halves(jnp.concatenate([held["q", c], maps[c]], axis=1))
        both = dot_n(left, jnp.concatenate([pair_rows(t, c) for t in (m1, m2, m1)], axis=0))
        gu, g = both[:STEP, : total + LANES], both[:STEP, total + LANES :]
        nu, d = both[STEP:, : total + LANES], both[STEP:, total + LANES :]
        g1, g2 = halves(g)
        n1, n2 = halves(nu)
        z = dot_0(jnp.concatenate([g1, g1, g2], axis=0), jnp.concatenate([n1, n2, n1], axis=0))
        z = jnp.concatenate([held["z", c] + z[: size - STEP], z[size - STEP :]], axis=0)
        energy = held["lib", c] + jnp.sum(gu * nu, axis=0, keepdims=True)
        w = held["sum", c][:, :total] + jnp.sum(
            jnp.concatenate([gu[:, total:]] * (total // LANES), axis=1) * nu[:, :total], axis=0, keepdims=True
        )
        kd = thirds(g * d)
        kd = dot_0(jnp.concatenate(kd, axis=0), jnp.ones((3 * STEP, LANES), BF16))
        kd = kd + jnp.concatenate(held["diag", c], axis=0)
        p = z[:, total:]
        s = energy[:, total:]
        s = jnp.where(s > 0.0, 1.0 / jnp.where(s > 0.0, s, 1.0), 0.0)
        ws = w * s[:, 0:1]
        lib = (held["norm"] - energy[:, :total] + w * ws) * (1.0 / RIDGE)
        lib = 1.0 / (jnp.maximum(lib, 0.0) + EPS)
        kd = kd - p * p * s
        pix = n * (1.0 - (n * RIDGE) * kd) - 1.0
        gain = (n * n * bands) / (jnp.maximum(pix, 0.0) + EPS)
        pieces = []
        for i in range(0, total, LANES):
            e = z[:, i : i + LANES] - p * ws[:, i : i + LANES]
            pieces.append(e * e * gain * lib[:, i : i + LANES])
        res.append(jnp.concatenate(pieces, axis=1).reshape(devices, 1, CAP, total))
    joined = jnp.concatenate(res, axis=1).reshape(devices, OWNED * CAP, total).astype(BF16)
    for lo, hi in ((half, devices), (0, half)):
        outbound[lo:hi] = joined[lo:hi]
        for r in range(hi - 1, max(lo, 1) - 1, -1):
            back(r).start()
    returned[0] = outbound[0]
    for r in range(1, devices):
        tell(r).wait_send()
        go(r).wait_send()
    for cp in lends:
        cp.wait_send()
    for r in range(1, devices):
        back(r).wait()
    out_ref[...] = dot_n(take_ref[...], returned[...].reshape(size * OWNED, total)).astype(BF16)


def narrow(pixels, labels, targets):
    n_tile, n_grp = lax.axis_size("tile"), lax.axis_size("grp")
    devices = n_tile * n_grp
    rows, bands = pixels.shape
    total = targets.shape[0] * n_grp
    deep = (OWNED * (bands // LANES) + 1) * SUB
    vmem = pl.BlockSpec(memory_space=pltpu.VMEM)
    dma = pltpu.SemaphoreType.DMA
    return pl.pallas_call(
        functools.partial(step_body, bands, n_tile, n_grp),
        out_shape=jax.ShapeDtypeStruct((rows, total), BF16),
        in_specs=[vmem] * 3,
        out_specs=vmem,
        scratch_shapes=[
            pltpu.VMEM((devices, deep, LANES), BF16),
            pltpu.VMEM((devices, deep, LANES), BF16),
            pltpu.VMEM((devices, 1, LANES), F32),
            pltpu.VMEM((devices, 1, LANES), F32),
            pltpu.VMEM((n_grp, bands, targets.shape[0]), BF16),
            pltpu.VMEM((devices, OWNED * CAP, total), BF16),
            pltpu.VMEM((devices, OWNED * CAP, total), BF16),
            pltpu.VMEM((rows, NCLUST * CAP), BF16),
            dma((devices,)), dma((devices,)),
            dma((devices,)), dma((devices,)),
            dma((n_grp,)), dma((n_grp,)),
            dma((devices,)), dma((devices,)),
        ],
        compiler_params=pltpu.CompilerParams(
            collective_id=0, has_side_effects=True, vmem_limit_bytes=60 * 1024 * 1024
        ),
    )(labels.reshape(1, rows), pixels.T, targets.T)


def wide_cluster(pixels, labels, targets):
    n_tile = lax.axis_size("tile")
    n_grp = lax.axis_size("grp")
    band_count = pixels.shape[1]
    per_owner = 2 * NCLUST // n_tile
    target_total = targets.shape[0] * n_grp
    clusters = jnp.arange(NCLUST, dtype=jnp.int32)
    member = (labels[:, None] == clusters[None, :]).astype(jnp.int32)
    local_count = jnp.sum(member, axis=0).astype(jnp.float32)
    counts = lax.psum(local_count, ("tile", "grp"))
    place_rank = jnp.sum(jnp.cumsum(member, axis=0) * member, axis=1) - 1
    owner_pair = labels // per_owner
    inner_slot = labels % per_owner
    slot_width = CAP
    target_tile = 2 * owner_pair
    slot_index = (target_tile * per_owner + inner_slot) * slot_width + place_rank
    slot_total = n_tile * per_owner * slot_width
    outgoing = jnp.zeros((slot_total, band_count), jnp.bfloat16).at[slot_index].set(pixels)
    outgoing = outgoing.reshape(n_tile, per_owner * slot_width, band_count)
    arrived = lax.all_to_all(outgoing, "tile", split_axis=0, concat_axis=0, tiled=True)
    grouped = arrived.reshape(n_tile, per_owner, slot_width, band_count)
    gram_sum = jnp.einsum("scwb,scwd->cbd", grouped, grouped, preferred_element_type=jnp.float32)
    first_sums = jnp.sum(grouped, axis=(0, 2), dtype=jnp.float32)
    gram_sum, first_sums = lax.psum((gram_sum, first_sums), "grp")
    own_pair = lax.axis_index("tile") // 2
    own_counts = lax.dynamic_slice_in_dim(counts, own_pair * per_owner, per_owner, 0)
    own_counts = jnp.maximum(own_counts, 1.0)
    centre = first_sums / own_counts[:, None]
    identity = jnp.eye(band_count, dtype=jnp.float32)
    covariance = (
        gram_sum / own_counts[:, None, None]
        - centre[:, :, None] * centre[:, None, :]
        + 0.05 * identity
    )
    factor = jnp.linalg.cholesky(covariance)
    inverse = jax.scipy.linalg.solve_triangular(
        factor, jnp.broadcast_to(identity, factor.shape), lower=True
    )
    whitened = jnp.einsum(
        "tb,cdb->ctd",
        lax.all_gather(targets, "grp", axis=0, tiled=True).astype(jnp.float32),
        inverse,
        precision=lax.Precision.HIGHEST,
    )
    lib_norm = jnp.sum(whitened * whitened, axis=-1)
    centered = grouped.astype(jnp.float32) - centre[None, :, None, :]
    white_pix = jnp.einsum("scwb,cdb->scwd", centered, inverse, precision=lax.Precision.HIGHEST)
    inner_prod = jnp.einsum("scwd,ctd->scwt", white_pix, whitened, precision=lax.Precision.HIGHEST)
    pix_norm = jnp.sum(white_pix * white_pix, axis=-1)
    result = (
        band_count
        * inner_prod
        * inner_prod
        / ((lib_norm[None, :, None, :] + 1e-06) * (pix_norm[:, :, :, None] + 1e-06))
    )
    outbound = result.astype(jnp.bfloat16).reshape(n_tile, per_owner * slot_width, target_total)
    returned = lax.all_to_all(outbound, "tile", split_axis=0, concat_axis=0, tiled=True)
    flat_scores = returned.reshape(slot_total, target_total)
    return flat_scores[slot_index]


def local(pixels, labels, targets):
    n_tile, n_grp = lax.axis_size("tile"), lax.axis_size("grp")
    devices = n_tile * n_grp
    rest = pixels.shape[1] % LANES
    if (
        NCLUST == OWNED * devices
        and n_grp == 4
        and n_tile & (n_tile - 1) == 0
        and devices * CAP % (2 * STEP) == 0
        and rest % 16 == 0
        and OWNED * (rest + 1) <= LANES
    ):
        return narrow(pixels, labels, targets)
    return wide_cluster(pixels, labels, targets)


def solution(mesh):
    return jax.shard_map(
        local,
        mesh=mesh,
        in_specs=(P(("tile", "grp"), None), P(("tile", "grp")), P("grp", None)),
        out_specs=P(("tile", "grp"), None),
        check_vma=False,
    )
```

```python
import functools

import jax
import jax.numpy as jnp
from jax import lax
from jax.experimental import pallas as pl
from jax.experimental.pallas import tpu as pltpu
from jax.sharding import PartitionSpec as P

NCLUST = 64
CAP = 8
RIDGE = 0.05
EPS = 1e-06
STEP = 64
LANES = 128
SUB = 8
PIV = 4
OWNED = 2
MESH = pl.DeviceIdType.MESH
F32 = jnp.float32
BF16 = jnp.bfloat16


def dot_t(a, b):
    return lax.dot_general(a, b, (((1,), (1,)), ((), ())), preferred_element_type=F32)


def dot_0(a, b):
    return lax.dot_general(a, b, (((0,), (0,)), ((), ())), preferred_element_type=F32)


def dot_n(a, b):
    return lax.dot_general(a, b, (((1,), (0,)), ((), ())), preferred_element_type=F32)


def halves(v):
    big = v.astype(BF16)
    return big, (v - big.astype(F32)).astype(BF16)


def thirds(v):
    big, rest = v.astype(BF16), v
    rest = rest - big.astype(F32)
    mid = rest.astype(BF16)
    return big, mid, (rest - mid.astype(F32)).astype(BF16)


def six_left(t, axis):
    return jnp.concatenate([t[0], t[0], t[1], t[0], t[1], t[2]], axis=axis)


def six_right(t, axis):
    return jnp.concatenate([t[0], t[1], t[0], t[2], t[1], t[0]], axis=axis)


def pair_rows(t, c):
    zero = jnp.zeros_like(t)
    return jnp.concatenate([zero] * c + [t] + [zero] * (OWNED - 1 - c), axis=0)


def grow(v, rows, width):
    if v.shape[1] < width:
        v = jnp.concatenate([v, jnp.zeros((v.shape[0], width - v.shape[1]), v.dtype)], axis=1)
    if v.shape[0] < rows:
        v = jnp.concatenate([v, jnp.zeros((rows - v.shape[0], v.shape[1]), v.dtype)], axis=0)
    return v


def pivot_inverse(e):
    r = 1.0 / (e[0][0] * e[1][1] - e[0][1] * e[0][1])
    i00, i01, i11 = e[1][1] * r, -e[0][1] * r, e[0][0] * r
    x00 = i00 * e[0][2] + i01 * e[1][2]
    x01 = i00 * e[0][3] + i01 * e[1][3]
    x10 = i01 * e[0][2] + i11 * e[1][2]
    x11 = i01 * e[0][3] + i11 * e[1][3]
    s00 = e[2][2] - (e[0][2] * x00 + e[1][2] * x10)
    s01 = e[2][3] - (e[0][2] * x01 + e[1][2] * x11)
    s11 = e[3][3] - (e[0][3] * x01 + e[1][3] * x11)
    q = 1.0 / (s00 * s11 - s01 * s01)
    t00, t01, t11 = s11 * q, -s01 * q, s00 * q
    y00 = -(x00 * t00 + x01 * t01)
    y01 = -(x00 * t01 + x01 * t11)
    y10 = -(x10 * t00 + x11 * t01)
    y11 = -(x10 * t01 + x11 * t11)
    n00 = i00 - (y00 * x00 + y01 * x01)
    n01 = i01 - (y00 * x10 + y01 * x11)
    n11 = i11 - (y10 * x10 + y11 * x11)
    return [[n00, n01, y00, y01], [n01, n11, y10, y11], [y00, y10, t00, t01], [y01, y11, t01, t11]]


def paired_factor(tile, fill):
    rows = tile.shape[0]
    lanes = lax.broadcasted_iota(jnp.int32, (SUB, LANES), 1)
    sub = lax.broadcasted_iota(jnp.int32, (SUB, LANES), 0)
    base = jnp.where(lanes < STEP, 0, STEP)
    inside = lanes - base
    parts = [tile[g : g + SUB] for g in range(0, rows, SUB)]
    low, scaled = [], []
    for j in range(0, rows, PIV):
        home, at = j // SUB, j % SUB
        pick = lambda p: [jnp.take_along_axis(p, base + (j + c), axis=1) for c in range(PIV)]
        spread = lambda v, a: jnp.broadcast_to(v[at + a : at + a + 1, :], (SUB, LANES))
        first = pick(parts[home])
        inv = pivot_inverse([[spread(first[c], a) if a <= c else None for c in range(PIV)] for a in range(PIV)])
        block = (inside >= j) & (inside < j + PIV)
        src = [jnp.where(block, jnp.where(inside == j + c, 1.0, 0.0), spread(parts[home], c)) for c in range(PIV)]
        norm = [(inv[a][0] * src[0] + inv[a][1] * src[1]) + (inv[a][2] * src[2] + inv[a][3] * src[3]) for a in range(PIV)]
        if not at:
            low.append(jnp.zeros((SUB, LANES), F32))
            scaled.append(jnp.zeros((SUB, LANES), F32))
        done = inside < j + PIV
        for a in range(PIV):
            here = (sub == at + a) & done
            low[home] = jnp.where(here, src[a], low[home])
            scaled[home] = jnp.where(here, norm[a], scaled[home])
        for g in range(home if at + PIV < SUB else home + 1, rows // SUB):
            col = first if g == home else pick(parts[g])
            parts[g] = jnp.where(block, 0.0, parts[g]) - (
                (col[0] * norm[0] + col[1] * norm[1]) + (col[2] * norm[2] + col[3] * norm[3])
            )
        if fill:
            fill.pop(0)()
    while fill:
        fill.pop(0)()
    return jnp.concatenate(low + scaled, axis=0)


class Eliminate:
    def __init__(self):
        self.inverse = [None] * OWNED
        self.k = 0

    def reduce(self, rows):
        k = self.k
        wide = rows[0].shape[1]
        old = -(-k * STEP // LANES) * LANES
        lane = lax.broadcasted_iota(jnp.int32, (STEP, LANES), 1)
        own = [m[:, k * STEP // LANES * LANES :][:, :LANES] for m in rows]
        odd = k % 2
        own[1 - odd] = pltpu.roll(own[1 - odd], STEP, 1)
        pair = jnp.where(lane < STEP, own[0], own[1])
        wl = lax.broadcasted_iota(jnp.int32, (STEP, wide), 1)
        ws = lax.broadcasted_iota(jnp.int32, (STEP, wide), 0)
        eye = jnp.where(wl == ws + k * STEP, 1.0, 0.0)
        if not k:
            return pair, [eye] * OWNED
        lefts, rights, maps = [], [], []
        for c, m in enumerate(rows):
            r3 = thirds(m[:, :old])
            lift = dot_n(six_left(r3, 1), six_right(thirds(self.inverse[c]), 0))
            maps.append(eye - grow(lift, STEP, wide))
            lefts.append(six_left(thirds(lift), 1))
            rights.append(six_right([pair_rows(t, c) for t in r3], 1))
        return pair - dot_t(jnp.concatenate(lefts, axis=1), jnp.concatenate(rights, axis=1)), maps

    def extend(self, factor, maps):
        wide = maps[0].shape[1]
        lane = lax.broadcasted_iota(jnp.int32, factor.shape, 1)
        left = None if not self.k else six_left(thirds(factor), 1)
        for c in range(OWNED):
            if not self.k:
                both = factor if not c else pltpu.roll(factor, STEP, 1)
                both = jnp.where(lane < STEP, both, 0.0)
            else:
                q3 = thirds(maps[c])
                both = dot_n(left, six_right([pair_rows(t, c) for t in q3], 0))
            upd = dot_0(six_left(thirds(both[:STEP]), 0), six_right(thirds(both[STEP:]), 0))
            self.inverse[c] = upd if not self.k else grow(self.inverse[c], wide, wide) + upd
        self.k += 1


def slot_of(lab, me, devices):
    count = lab.shape[1]
    ri = lax.broadcasted_iota(jnp.int32, (count, count), 0)
    ci = lax.broadcasted_iota(jnp.int32, (count, count), 1)
    lab_row = lab.astype(F32)
    lab_col = jnp.sum(jnp.where(ri == ci, lab_row, 0.0), axis=1, keepdims=True)
    same = jnp.where(lab_row == lab_col, 1.0, 0.0)
    rank_col = jnp.sum(jnp.where(ci < ri, same, 0.0), axis=1, keepdims=True).astype(jnp.int32)
    rank_row = jnp.sum(jnp.where(ri < ci, same, 0.0), axis=0, keepdims=True).astype(jnp.int32)
    lab_col = lab_col.astype(jnp.int32)
    hop = lambda v: jnp.bitwise_xor(lax.shift_right_logical(v, 1), me)
    side = lambda v: jnp.bitwise_and(v, 1)
    slots = devices * CAP
    down = lax.broadcasted_iota(jnp.int32, (slots, count), 0)
    put = [
        jnp.where(down == jnp.where(side(lab) == c, hop(lab) * CAP + rank_row, -1), 1.0, 0.0).astype(BF16)
        for c in range(OWNED)
    ]
    across = lax.broadcasted_iota(jnp.int32, (count, slots * OWNED), 1)
    take = jnp.where(across == (hop(lab_col) * OWNED + side(lab_col)) * CAP + rank_col, 1.0, 0.0).astype(BF16)
    far = lax.broadcasted_iota(jnp.int32, (devices, count), 0)
    lane = lax.broadcasted_iota(jnp.int32, (count, LANES), 1)
    near = jnp.where(lax.div(lane, STEP) == side(lab_col), 1.0, 0.0).astype(BF16)
    tally = dot_n(jnp.where(far == hop(lab), 1.0, 0.0).astype(BF16), near)
    return take, put, tally


def step_body(
    bands, n_tile, n_grp,
    lab_in, pix_in, tgt_in, out_ref,
    lab_ref, pix_ref, tgt_ref, outgoing, arrived, counts, heard, library, outbound, returned, take_ref,
    load_sem, send_n, recv_n, send_a, recv_a, send_t, recv_t, send_b, recv_b,
):
    devices = n_tile * n_grp
    full, rest = bands // LANES, bands % LANES
    flag = OWNED * rest
    total = outbound.shape[2]
    size = devices * CAP
    blocks = size // STEP
    span = STEP // CAP
    tile = lax.axis_index("tile")
    grp = lax.axis_index("grp")
    me = tile * n_grp + grp

    def flip(v, r):
        out = v
        for k in range(r.bit_length()):
            if (r >> k) & 1:
                out = out + (1 - 2 * lax.rem(lax.div(v, 1 << k), 2)) * (1 << k)
        return out

    def place(r):
        return (flip(tile, r // n_grp), flip(grp, r % n_grp))

    barrier = pltpu.get_barrier_semaphore()
    for r in range(devices - 1, 0, -1):
        pl.semaphore_signal(barrier, inc=1, device_id=place(r), device_id_type=MESH)

    pulls = [
        pltpu.make_async_copy(src, dst, load_sem.at[i])
        for i, (src, dst) in enumerate(((lab_in, lab_ref), (pix_in, pix_ref), (tgt_in, tgt_ref)))
    ]
    for cp in pulls:
        cp.start()
    for cp in pulls:
        cp.wait()
    take, put, tally = slot_of(lab_ref[...], me, devices)
    take_ref[...] = take
    counts[...] = tally.reshape(devices, 1, LANES)
    heard[0] = counts[0]
    for c in range(OWNED):
        body = dot_t(put[c], pix_ref[: full * LANES, :])
        for t in range(full):
            at = (c * full + t) * SUB
            outgoing[:, at : at + SUB, :] = body[:, t * LANES : (t + 1) * LANES].astype(BF16).reshape(devices, SUB, LANES)
    tail = pix_ref[full * LANES :, :]
    pad = LANES - flag
    mark = lax.broadcasted_iota(jnp.int32, (pad, tail.shape[1]), 0)
    ends = [
        jnp.concatenate(
            [tail if i == c else jnp.zeros_like(tail) for i in range(OWNED)]
            + [jnp.where(mark == c, 1.0, 0.0).astype(BF16)],
            axis=0,
        )
        for c in range(OWNED)
    ]
    ends = dot_t(jnp.concatenate(put, axis=1), jnp.concatenate(ends, axis=1))
    outgoing[:, OWNED * full * SUB :, :] = ends.astype(BF16).reshape(devices, SUB, LANES)
    arrived[0] = outgoing[0]
    library[grp] = tgt_ref[...]
    pl.semaphore_wait(barrier, devices - 1)

    def ship(src, dst, sends, recvs, r):
        return pltpu.make_async_remote_copy(
            src_ref=src.at[r], dst_ref=dst.at[r],
            send_sem=sends.at[r], recv_sem=recvs.at[r],
            device_id=place(r), device_id_type=MESH,
        )

    tell = lambda r: ship(counts, heard, send_n, recv_n, r)
    go = lambda r: ship(outgoing, arrived, send_a, recv_a, r)
    back = lambda r: ship(outbound, returned, send_b, recv_b, r)

    def lend(i, src, home, to):
        return pltpu.make_async_remote_copy(
            src_ref=src, dst_ref=library.at[home], send_sem=send_t.at[i], recv_sem=recv_t.at[i],
            device_id=(tile, flip(grp, to)), device_id_type=MESH,
        )

    across = flip(grp, 2)
    lends = [lend(0, tgt_ref, grp, 1), lend(1, tgt_ref, grp, 2), lend(2, library.at[across], across, 1)]
    half = devices // 2
    for r in range(devices - 1, 0, -1):
        tell(r).start()
    for i in range(half):
        go(half + i).start()
        for r in (4 * i + 1, 4 * i + 2, 4 * i + 3, 4 * i + 4):
            if r < half:
                go(r).start()
    lends[0].start()
    lends[1].start()

    lane = lax.broadcasted_iota(jnp.int32, (STEP, LANES), 1)
    own = [((lane >= c * rest) & (lane < (c + 1) * rest)) for c in range(OWNED)]
    kept = [own[c] | (lane == flag + c) for c in range(OWNED)]
    sign = lax.broadcasted_iota(jnp.int32, (16, (full + 1) * LANES), 1)
    sign = [jnp.where(sign == full * LANES + flag + c, 1.0, 0.0).astype(BF16) for c in range(OWNED)]
    lefts = [[] for _ in range(OWNED)]
    rights = [[] for _ in range(OWNED)]
    valid = [[] for _ in range(OWNED)]
    centre = [None] * OWNED
    state = Eliminate()
    number = None
    held = {}

    def load(b):
        arr = arrived[b * span : (b + 1) * span].astype(F32)
        cut = lambda i: arr[:, i * SUB : (i + 1) * SUB, :].reshape(STEP, LANES)
        edge = cut(OWNED * full)
        out = []
        for c in range(OWNED):
            main = [cut(c * full + t) for t in range(full)]
            x = jnp.concatenate(main + [edge], axis=1)
            if b == 0:
                tops = jnp.maximum(jnp.sum(edge[:, flag + c : flag + c + 1]), 1.0)
                mid = jnp.concatenate(main + [jnp.where(own[c], edge, 0.0)], axis=1)
                mid = jnp.sum(mid, axis=0, keepdims=True) * (1.0 / tops)
                mid = mid.astype(BF16)
                centre[c] = (mid, mid.astype(F32))
            lefts[c].append(x.astype(BF16))
            rights[c].append(jnp.concatenate(main + [jnp.where(kept[c], edge, 0.0)], axis=1).astype(BF16))
            valid[c].append(edge[:, flag + c : flag + c + 1])
            out.append(jnp.sum(x * centre[c][1], axis=1, keepdims=True))
        return out

    def gram(b, lean):
        rows = []
        wide = -(-(b + 1) * STEP // LANES) * LANES
        for c in range(OWNED):
            mid, midf = centre[c]
            left = jnp.concatenate([lefts[c][b], jnp.broadcast_to(mid, (16, mid.shape[1])), sign[c]], axis=0)
            right = jnp.concatenate(rights[c], axis=0)
            if right.shape[0] < wide:
                right = jnp.concatenate([right, jnp.zeros((wide - right.shape[0], right.shape[1]), BF16)], axis=0)
            g = dot_t(left, right)
            along, has = g[STEP : STEP + 1], g[STEP + 16 : STEP + 17]
            along = along - jnp.sum(midf * midf) * has
            rows.append(g[:STEP] - valid[c][b] * along - lean[c] * has)
        return rows

    def scale(b, rows):
        wide = rows[0].shape[1]
        wl = lax.broadcasted_iota(jnp.int32, (STEP, wide), 1)
        ws = lax.broadcasted_iota(jnp.int32, (STEP, wide), 0)
        diag = wl == ws + b * STEP
        return [m + jnp.where(diag, number[c] * RIDGE, 0.0) for c, m in enumerate(rows)]

    def fetch(b):
        for r in range(max(b * span, 1), (b + 1) * span):
            go(r).wait_recv()
        return load(b)

    def measure(c):
        def run():
            lib = [held["lib"][: full * LANES]]
            lib += [held["lib"][full * LANES :] if i == c else jnp.zeros((rest, total), BF16) for i in range(OWNED)]
            lib += [jnp.zeros((pad, total), BF16)]
            u = dot_n(jnp.concatenate(lefts[c], axis=0), jnp.concatenate(lib, axis=0))
            v = jnp.concatenate(valid[c], axis=0)
            u = (u - jnp.sum(u, axis=0, keepdims=True) * (1.0 / number[c])) * v
            held[c] = jnp.concatenate([u, jnp.broadcast_to(v, (size, LANES))], axis=1)

        return run

    def advance(c):
        def run():
            u1, u2 = halves(held[c])
            m1, m2 = halves(jnp.concatenate([state.inverse[c][: size - STEP], held["maps"][c]], axis=0))
            z = dot_n(jnp.concatenate([m1, m1, m2], axis=1), jnp.concatenate([u1, u2, u1], axis=0))
            held["z", c] = z[: size - STEP]
            held["q", c] = z[size - STEP :]

        return run

    def summarise(c):
        def run():
            z = held["z", c]
            held["lib", c] = jnp.sum(held[c][: size - STEP] * z, axis=0, keepdims=True)
            held["sum", c] = jnp.sum(z, axis=0, keepdims=True)
            inv = state.inverse[c]
            held["diag", c] = [
                jnp.sum(jnp.where(diag, inv[i : i + LANES, i : i + LANES], 0.0), axis=1, keepdims=True)
                for i in range(0, size, LANES)
            ]

        return run

    def squares():
        tf = held["lib"].astype(F32)
        held["norm"] = jnp.sum(tf * tf, axis=0, keepdims=True)

    diag = lax.broadcasted_iota(jnp.int32, (LANES, LANES), 0) == lax.broadcasted_iota(jnp.int32, (LANES, LANES), 1)
    rows = gram(0, fetch(0))
    for r in range(1, devices):
        tell(r).wait_recv()
    heads = jnp.maximum(jnp.sum(heard[...], axis=0), 1.0)
    number = [heads[:, c * STEP : c * STEP + 1] for c in range(OWNED)]
    for b in range(blocks):
        pair, maps = state.reduce(scale(b, rows))
        if b < blocks - 1:
            factor = paired_factor(pair, [])
            state.extend(factor, maps)
            lean = fetch(b + 1)
            rows = gram(b + 1, lean)
            if not b:
                lends[1].wait_recv()
                lends[2].start()
    held["maps"] = maps
    for i in (0, 2):
        lends[i].wait_recv()
    held["lib"] = jnp.concatenate([library[i] for i in range(n_grp)], axis=1)
    state.inverse = [grow(m, size, size) for m in state.inverse]
    fill = [measure(0), measure(1), squares, advance(0), advance(1), summarise(0), summarise(1)]
    factor = paired_factor(pair, fill)

    f1, f2 = halves(factor)
    left = jnp.concatenate([f1, f1, f2], axis=1)
    res = []
    for c in range(OWNED):
        n = number[c]
        m1, m2 = halves(jnp.concatenate([held["q", c], maps[c]], axis=1))
        both = dot_n(left, jnp.concatenate([pair_rows(t, c) for t in (m1, m2, m1)], axis=0))
        gu, g = both[:STEP, : total + LANES], both[:STEP, total + LANES :]
        nu, d = both[STEP:, : total + LANES], both[STEP:, total + LANES :]
        g1, g2 = halves(g)
        n1, n2 = halves(nu)
        z = dot_0(jnp.concatenate([g1, g1, g2], axis=0), jnp.concatenate([n1, n2, n1], axis=0))
        z = jnp.concatenate([held["z", c] + z[: size - STEP], z[size - STEP :]], axis=0)
        energy = held["lib", c] + jnp.sum(gu * nu, axis=0, keepdims=True)
        w = held["sum", c][:, :total] + jnp.sum(
            jnp.concatenate([gu[:, total:]] * (total // LANES), axis=1) * nu[:, :total], axis=0, keepdims=True
        )
        kd = thirds(g * d)
        kd = dot_0(jnp.concatenate(kd, axis=0), jnp.ones((3 * STEP, LANES), BF16))
        kd = kd + jnp.concatenate(held["diag", c], axis=0)
        p = z[:, total:]
        s = energy[:, total:]
        s = jnp.where(s > 0.0, 1.0 / jnp.where(s > 0.0, s, 1.0), 0.0)
        ws = w * s[:, 0:1]
        lib = (held["norm"] - energy[:, :total] + w * ws) * (1.0 / RIDGE)
        lib = 1.0 / (jnp.maximum(lib, 0.0) + EPS)
        kd = kd - p * p * s
        pix = n * (1.0 - (n * RIDGE) * kd) - 1.0
        gain = (n * n * bands) / (jnp.maximum(pix, 0.0) + EPS)
        pieces = []
        for i in range(0, total, LANES):
            e = z[:, i : i + LANES] - p * ws[:, i : i + LANES]
            pieces.append(e * e * gain * lib[:, i : i + LANES])
        res.append(jnp.concatenate(pieces, axis=1).reshape(devices, 1, CAP, total))
    joined = jnp.concatenate(res, axis=1).reshape(devices, OWNED * CAP, total).astype(BF16)
    outbound[...] = joined
    for i in range(half):
        back(half + i).start()
        if i:
            back(i).start()
    returned[0] = outbound[0]
    for r in range(1, devices):
        tell(r).wait_send()
        go(r).wait_send()
    for cp in lends:
        cp.wait_send()
    for r in range(1, devices):
        back(r).wait()
    out_ref[...] = dot_n(take_ref[...], returned[...].reshape(size * OWNED, total)).astype(BF16)


def narrow(pixels, labels, targets):
    n_tile, n_grp = lax.axis_size("tile"), lax.axis_size("grp")
    devices = n_tile * n_grp
    rows, bands = pixels.shape
    total = targets.shape[0] * n_grp
    deep = (OWNED * (bands // LANES) + 1) * SUB
    vmem = pl.BlockSpec(memory_space=pltpu.VMEM)
    dma = pltpu.SemaphoreType.DMA
    return pl.pallas_call(
        functools.partial(step_body, bands, n_tile, n_grp),
        out_shape=jax.ShapeDtypeStruct((rows, total), BF16),
        in_specs=[pl.BlockSpec(memory_space=pl.ANY)] * 3,
        out_specs=vmem,
        scratch_shapes=[
            pltpu.VMEM((1, rows), labels.dtype),
            pltpu.VMEM((bands, rows), BF16),
            pltpu.VMEM((bands, targets.shape[0]), BF16),
            pltpu.VMEM((devices, deep, LANES), BF16),
            pltpu.VMEM((devices, deep, LANES), BF16),
            pltpu.VMEM((devices, 1, LANES), F32),
            pltpu.VMEM((devices, 1, LANES), F32),
            pltpu.VMEM((n_grp, bands, targets.shape[0]), BF16),
            pltpu.VMEM((devices, OWNED * CAP, total), BF16),
            pltpu.VMEM((devices, OWNED * CAP, total), BF16),
            pltpu.VMEM((rows, NCLUST * CAP), BF16),
            dma((3,)),
            dma((devices,)), dma((devices,)),
            dma((devices,)), dma((devices,)),
            dma((n_grp,)), dma((n_grp,)),
            dma((devices,)), dma((devices,)),
        ],
        compiler_params=pltpu.CompilerParams(
            collective_id=0, has_side_effects=True, vmem_limit_bytes=60 * 1024 * 1024
        ),
    )(labels.reshape(1, rows), pixels.T, targets.T)


def wide_cluster(pixels, labels, targets):
    n_tile = lax.axis_size("tile")
    n_grp = lax.axis_size("grp")
    band_count = pixels.shape[1]
    per_owner = 2 * NCLUST // n_tile
    target_total = targets.shape[0] * n_grp
    clusters = jnp.arange(NCLUST, dtype=jnp.int32)
    member = (labels[:, None] == clusters[None, :]).astype(jnp.int32)
    local_count = jnp.sum(member, axis=0).astype(jnp.float32)
    counts = lax.psum(local_count, ("tile", "grp"))
    place_rank = jnp.sum(jnp.cumsum(member, axis=0) * member, axis=1) - 1
    owner_pair = labels // per_owner
    inner_slot = labels % per_owner
    slot_width = CAP
    target_tile = 2 * owner_pair
    slot_index = (target_tile * per_owner + inner_slot) * slot_width + place_rank
    slot_total = n_tile * per_owner * slot_width
    outgoing = jnp.zeros((slot_total, band_count), jnp.bfloat16).at[slot_index].set(pixels)
    outgoing = outgoing.reshape(n_tile, per_owner * slot_width, band_count)
    arrived = lax.all_to_all(outgoing, "tile", split_axis=0, concat_axis=0, tiled=True)
    grouped = arrived.reshape(n_tile, per_owner, slot_width, band_count)
    gram_sum = jnp.einsum("scwb,scwd->cbd", grouped, grouped, preferred_element_type=jnp.float32)
    first_sums = jnp.sum(grouped, axis=(0, 2), dtype=jnp.float32)
    gram_sum, first_sums = lax.psum((gram_sum, first_sums), "grp")
    own_pair = lax.axis_index("tile") // 2
    own_counts = lax.dynamic_slice_in_dim(counts, own_pair * per_owner, per_owner, 0)
    own_counts = jnp.maximum(own_counts, 1.0)
    centre = first_sums / own_counts[:, None]
    identity = jnp.eye(band_count, dtype=jnp.float32)
    covariance = (
        gram_sum / own_counts[:, None, None]
        - centre[:, :, None] * centre[:, None, :]
        + 0.05 * identity
    )
    factor = jnp.linalg.cholesky(covariance)
    inverse = jax.scipy.linalg.solve_triangular(
        factor, jnp.broadcast_to(identity, factor.shape), lower=True
    )
    whitened = jnp.einsum(
        "tb,cdb->ctd",
        lax.all_gather(targets, "grp", axis=0, tiled=True).astype(jnp.float32),
        inverse,
        precision=lax.Precision.HIGHEST,
    )
    lib_norm = jnp.sum(whitened * whitened, axis=-1)
    centered = grouped.astype(jnp.float32) - centre[None, :, None, :]
    white_pix = jnp.einsum("scwb,cdb->scwd", centered, inverse, precision=lax.Precision.HIGHEST)
    inner_prod = jnp.einsum("scwd,ctd->scwt", white_pix, whitened, precision=lax.Precision.HIGHEST)
    pix_norm = jnp.sum(white_pix * white_pix, axis=-1)
    result = (
        band_count
        * inner_prod
        * inner_prod
        / ((lib_norm[None, :, None, :] + 1e-06) * (pix_norm[:, :, :, None] + 1e-06))
    )
    outbound = result.astype(jnp.bfloat16).reshape(n_tile, per_owner * slot_width, target_total)
    returned = lax.all_to_all(outbound, "tile", split_axis=0, concat_axis=0, tiled=True)
    flat_scores = returned.reshape(slot_total, target_total)
    return flat_scores[slot_index]


def local(pixels, labels, targets):
    n_tile, n_grp = lax.axis_size("tile"), lax.axis_size("grp")
    devices = n_tile * n_grp
    rest = pixels.shape[1] % LANES
    if (
        NCLUST == OWNED * devices
        and n_grp == 4
        and n_tile & (n_tile - 1) == 0
        and devices * CAP % (2 * STEP) == 0
        and rest % 16 == 0
        and OWNED * (rest + 1) <= LANES
    ):
        return narrow(pixels, labels, targets)
    return wide_cluster(pixels, labels, targets)


def solution(mesh):
    return jax.shard_map(
        local,
        mesh=mesh,
        in_specs=(P(("tile", "grp"), None), P(("tile", "grp")), P("grp", None)),
        out_specs=P(("tile", "grp"), None),
        check_vma=False,
    )
```

```python
import functools

import jax
import jax.numpy as jnp
from jax import lax
from jax.experimental import pallas as pl
from jax.experimental.pallas import tpu as pltpu
from jax.sharding import PartitionSpec as P

NCLUST = 64
CAP = 8
RIDGE = 0.05
EPS = 1e-06
STEP = 64
LANES = 128
SUB = 8
PIV = 4
OWNED = 2
MESH = pl.DeviceIdType.MESH
F32 = jnp.float32
BF16 = jnp.bfloat16


def dot_t(a, b):
    return lax.dot_general(a, b, (((1,), (1,)), ((), ())), preferred_element_type=F32)


def dot_0(a, b):
    return lax.dot_general(a, b, (((0,), (0,)), ((), ())), preferred_element_type=F32)


def dot_n(a, b):
    return lax.dot_general(a, b, (((1,), (0,)), ((), ())), preferred_element_type=F32)


def halves(v):
    big = v.astype(BF16)
    return big, (v - big.astype(F32)).astype(BF16)


def thirds(v):
    big, rest = v.astype(BF16), v
    rest = rest - big.astype(F32)
    mid = rest.astype(BF16)
    return big, mid, (rest - mid.astype(F32)).astype(BF16)


def six_left(t, axis):
    return jnp.concatenate([t[0], t[0], t[1], t[0], t[1], t[2]], axis=axis)


def six_right(t, axis):
    return jnp.concatenate([t[0], t[1], t[0], t[2], t[1], t[0]], axis=axis)


def pair_rows(t, c):
    zero = jnp.zeros_like(t)
    return jnp.concatenate([zero] * c + [t] + [zero] * (OWNED - 1 - c), axis=0)


def grow(v, rows, width):
    if v.shape[1] < width:
        v = jnp.concatenate([v, jnp.zeros((v.shape[0], width - v.shape[1]), v.dtype)], axis=1)
    if v.shape[0] < rows:
        v = jnp.concatenate([v, jnp.zeros((rows - v.shape[0], v.shape[1]), v.dtype)], axis=0)
    return v


def pivot_inverse(e):
    r = 1.0 / (e[0][0] * e[1][1] - e[0][1] * e[0][1])
    i00, i01, i11 = e[1][1] * r, -e[0][1] * r, e[0][0] * r
    x00 = i00 * e[0][2] + i01 * e[1][2]
    x01 = i00 * e[0][3] + i01 * e[1][3]
    x10 = i01 * e[0][2] + i11 * e[1][2]
    x11 = i01 * e[0][3] + i11 * e[1][3]
    s00 = e[2][2] - (e[0][2] * x00 + e[1][2] * x10)
    s01 = e[2][3] - (e[0][2] * x01 + e[1][2] * x11)
    s11 = e[3][3] - (e[0][3] * x01 + e[1][3] * x11)
    q = 1.0 / (s00 * s11 - s01 * s01)
    t00, t01, t11 = s11 * q, -s01 * q, s00 * q
    y00 = -(x00 * t00 + x01 * t01)
    y01 = -(x00 * t01 + x01 * t11)
    y10 = -(x10 * t00 + x11 * t01)
    y11 = -(x10 * t01 + x11 * t11)
    n00 = i00 - (y00 * x00 + y01 * x01)
    n01 = i01 - (y00 * x10 + y01 * x11)
    n11 = i11 - (y10 * x10 + y11 * x11)
    return [[n00, n01, y00, y01], [n01, n11, y10, y11], [y00, y10, t00, t01], [y01, y11, t01, t11]]


def paired_factor(tile, fill):
    rows = tile.shape[0]
    lanes = lax.broadcasted_iota(jnp.int32, (SUB, LANES), 1)
    sub = lax.broadcasted_iota(jnp.int32, (SUB, LANES), 0)
    base = jnp.where(lanes < STEP, 0, STEP)
    inside = lanes - base
    parts = [tile[g : g + SUB] for g in range(0, rows, SUB)]
    low, scaled = [], []
    for j in range(0, rows, PIV):
        home, at = j // SUB, j % SUB
        pick = lambda p: [jnp.take_along_axis(p, base + (j + c), axis=1) for c in range(PIV)]
        spread = lambda v, a: jnp.broadcast_to(v[at + a : at + a + 1, :], (SUB, LANES))
        first = pick(parts[home])
        inv = pivot_inverse([[spread(first[c], a) if a <= c else None for c in range(PIV)] for a in range(PIV)])
        block = (inside >= j) & (inside < j + PIV)
        src = [jnp.where(block, jnp.where(inside == j + c, 1.0, 0.0), spread(parts[home], c)) for c in range(PIV)]
        norm = [(inv[a][0] * src[0] + inv[a][1] * src[1]) + (inv[a][2] * src[2] + inv[a][3] * src[3]) for a in range(PIV)]
        if not at:
            low.append(jnp.zeros((SUB, LANES), F32))
            scaled.append(jnp.zeros((SUB, LANES), F32))
        done = inside < j + PIV
        for a in range(PIV):
            here = (sub == at + a) & done
            low[home] = jnp.where(here, src[a], low[home])
            scaled[home] = jnp.where(here, norm[a], scaled[home])
        for g in range(home if at + PIV < SUB else home + 1, rows // SUB):
            col = first if g == home else pick(parts[g])
            parts[g] = jnp.where(block, 0.0, parts[g]) - (
                (col[0] * norm[0] + col[1] * norm[1]) + (col[2] * norm[2] + col[3] * norm[3])
            )
        if fill:
            fill.pop(0)()
    while fill:
        fill.pop(0)()
    return jnp.concatenate(low + scaled, axis=0)


class Eliminate:
    def __init__(self):
        self.inverse = [None] * OWNED
        self.k = 0

    def reduce(self, rows):
        k = self.k
        wide = rows[0].shape[1]
        old = -(-k * STEP // LANES) * LANES
        lane = lax.broadcasted_iota(jnp.int32, (STEP, LANES), 1)
        own = [m[:, k * STEP // LANES * LANES :][:, :LANES] for m in rows]
        odd = k % 2
        own[1 - odd] = pltpu.roll(own[1 - odd], STEP, 1)
        pair = jnp.where(lane < STEP, own[0], own[1])
        wl = lax.broadcasted_iota(jnp.int32, (STEP, wide), 1)
        ws = lax.broadcasted_iota(jnp.int32, (STEP, wide), 0)
        eye = jnp.where(wl == ws + k * STEP, 1.0, 0.0)
        if not k:
            return pair, [eye] * OWNED
        lefts, rights, maps = [], [], []
        for c, m in enumerate(rows):
            r3 = thirds(m[:, :old])
            lift = dot_n(six_left(r3, 1), six_right(thirds(self.inverse[c]), 0))
            maps.append(eye - grow(lift, STEP, wide))
            lefts.append(six_left(thirds(lift), 1))
            rights.append(six_right([pair_rows(t, c) for t in r3], 1))
        return pair - dot_t(jnp.concatenate(lefts, axis=1), jnp.concatenate(rights, axis=1)), maps

    def extend(self, factor, maps):
        wide = maps[0].shape[1]
        lane = lax.broadcasted_iota(jnp.int32, factor.shape, 1)
        left = None if not self.k else six_left(thirds(factor), 1)
        for c in range(OWNED):
            if not self.k:
                both = factor if not c else pltpu.roll(factor, STEP, 1)
                both = jnp.where(lane < STEP, both, 0.0)
            else:
                q3 = thirds(maps[c])
                both = dot_n(left, six_right([pair_rows(t, c) for t in q3], 0))
            upd = dot_0(six_left(thirds(both[:STEP]), 0), six_right(thirds(both[STEP:]), 0))
            self.inverse[c] = upd if not self.k else grow(self.inverse[c], wide, wide) + upd
        self.k += 1


def slot_of(lab, me, devices):
    count = lab.shape[1]
    ri = lax.broadcasted_iota(jnp.int32, (count, count), 0)
    ci = lax.broadcasted_iota(jnp.int32, (count, count), 1)
    lab_row = lab.astype(F32)
    lab_col = jnp.sum(jnp.where(ri == ci, lab_row, 0.0), axis=1, keepdims=True)
    same = jnp.where(lab_row == lab_col, 1.0, 0.0)
    rank_col = jnp.sum(jnp.where(ci < ri, same, 0.0), axis=1, keepdims=True).astype(jnp.int32)
    rank_row = jnp.sum(jnp.where(ri < ci, same, 0.0), axis=0, keepdims=True).astype(jnp.int32)
    lab_col = lab_col.astype(jnp.int32)
    hop = lambda v: jnp.bitwise_xor(lax.shift_right_logical(v, 1), me)
    side = lambda v: jnp.bitwise_and(v, 1)
    slots = devices * CAP
    down = lax.broadcasted_iota(jnp.int32, (slots, count), 0)
    put = [
        jnp.where(down == jnp.where(side(lab) == c, hop(lab) * CAP + rank_row, -1), 1.0, 0.0).astype(BF16)
        for c in range(OWNED)
    ]
    across = lax.broadcasted_iota(jnp.int32, (count, slots * OWNED), 1)
    take = jnp.where(across == (hop(lab_col) * OWNED + side(lab_col)) * CAP + rank_col, 1.0, 0.0).astype(BF16)
    far = lax.broadcasted_iota(jnp.int32, (devices, count), 0)
    lane = lax.broadcasted_iota(jnp.int32, (count, LANES), 1)
    near = jnp.where(lax.div(lane, STEP) == side(lab_col), 1.0, 0.0).astype(BF16)
    tally = dot_n(jnp.where(far == hop(lab), 1.0, 0.0).astype(BF16), near)
    return take, put, tally


def step_body(
    bands, n_tile, n_grp,
    lab_in, pix_in, tgt_in, out_ref,
    lab_ref, pix_ref, tgt_ref, outgoing, arrived, counts, heard, library, outbound, returned, take_ref,
    load_sem, send_n, recv_n, send_a, recv_a, send_t, recv_t, send_b, recv_b,
):
    devices = n_tile * n_grp
    full, rest = bands // LANES, bands % LANES
    flag = OWNED * rest
    total = outbound.shape[2]
    size = devices * CAP
    blocks = size // STEP
    span = STEP // CAP
    tile = lax.axis_index("tile")
    grp = lax.axis_index("grp")
    me = tile * n_grp + grp

    def flip(v, r):
        out = v
        for k in range(r.bit_length()):
            if (r >> k) & 1:
                out = out + (1 - 2 * lax.rem(lax.div(v, 1 << k), 2)) * (1 << k)
        return out

    def place(r):
        return (flip(tile, r // n_grp), flip(grp, r % n_grp))

    barrier = pltpu.get_barrier_semaphore()
    for r in range(devices - 1, 0, -1):
        pl.semaphore_signal(barrier, inc=1, device_id=place(r), device_id_type=MESH)

    pulls = [
        pltpu.make_async_copy(src, dst, load_sem.at[i])
        for i, (src, dst) in enumerate(((lab_in, lab_ref), (pix_in, pix_ref), (tgt_in, tgt_ref)))
    ]
    for cp in pulls:
        cp.start()
    for cp in pulls:
        cp.wait()
    take, put, tally = slot_of(lab_ref[...], me, devices)
    take_ref[...] = take
    counts[...] = tally.reshape(devices, 1, LANES)
    heard[0] = counts[0]
    for c in range(OWNED):
        body = dot_t(put[c], pix_ref[: full * LANES, :])
        for t in range(full):
            at = (c * full + t) * SUB
            outgoing[:, at : at + SUB, :] = body[:, t * LANES : (t + 1) * LANES].astype(BF16).reshape(devices, SUB, LANES)
    tail = pix_ref[full * LANES :, :]
    pad = LANES - flag
    mark = lax.broadcasted_iota(jnp.int32, (pad, tail.shape[1]), 0)
    ends = [
        jnp.concatenate(
            [tail if i == c else jnp.zeros_like(tail) for i in range(OWNED)]
            + [jnp.where(mark == c, 1.0, 0.0).astype(BF16)],
            axis=0,
        )
        for c in range(OWNED)
    ]
    ends = dot_t(jnp.concatenate(put, axis=1), jnp.concatenate(ends, axis=1))
    outgoing[:, OWNED * full * SUB :, :] = ends.astype(BF16).reshape(devices, SUB, LANES)
    arrived[0] = outgoing[0]
    library[grp] = tgt_ref[...]
    pl.semaphore_wait(barrier, devices - 1)

    def ship(src, dst, sends, recvs, r):
        return pltpu.make_async_remote_copy(
            src_ref=src.at[r], dst_ref=dst.at[r],
            send_sem=sends.at[r], recv_sem=recvs.at[r],
            device_id=place(r), device_id_type=MESH,
        )

    tell = lambda r: ship(counts, heard, send_n, recv_n, r)
    go = lambda r: ship(outgoing, arrived, send_a, recv_a, r)
    back = lambda r: ship(outbound, returned, send_b, recv_b, r)

    def lend(i, src, home, to):
        return pltpu.make_async_remote_copy(
            src_ref=src, dst_ref=library.at[home], send_sem=send_t.at[i], recv_sem=recv_t.at[i],
            device_id=(tile, flip(grp, to)), device_id_type=MESH,
        )

    across = flip(grp, 2)
    lends = [lend(0, tgt_ref, grp, 1), lend(1, tgt_ref, grp, 2), lend(2, library.at[across], across, 1)]
    half = devices // 2
    for r in range(devices - 1, 0, -1):
        tell(r).start()
    for i in range(half):
        for r in range(7 * i + 1, 7 * i + 8):
            if r < half:
                go(r).start()
        go(half + i).start()
        if i == 3:
            lends[0].start()
            lends[1].start()

    lane = lax.broadcasted_iota(jnp.int32, (STEP, LANES), 1)
    own = [((lane >= c * rest) & (lane < (c + 1) * rest)) for c in range(OWNED)]
    kept = [own[c] | (lane == flag + c) for c in range(OWNED)]
    sign = lax.broadcasted_iota(jnp.int32, (16, (full + 1) * LANES), 1)
    sign = [jnp.where(sign == full * LANES + flag + c, 1.0, 0.0).astype(BF16) for c in range(OWNED)]
    lefts = [[] for _ in range(OWNED)]
    rights = [[] for _ in range(OWNED)]
    valid = [[] for _ in range(OWNED)]
    centre = [None] * OWNED
    state = Eliminate()
    number = None
    held = {}

    def load(b):
        arr = arrived[b * span : (b + 1) * span].astype(F32)
        cut = lambda i: arr[:, i * SUB : (i + 1) * SUB, :].reshape(STEP, LANES)
        edge = cut(OWNED * full)
        out = []
        for c in range(OWNED):
            main = [cut(c * full + t) for t in range(full)]
            x = jnp.concatenate(main + [edge], axis=1)
            if b == 0:
                tops = jnp.maximum(jnp.sum(edge[:, flag + c : flag + c + 1]), 1.0)
                mid = jnp.concatenate(main + [jnp.where(own[c], edge, 0.0)], axis=1)
                mid = jnp.sum(mid, axis=0, keepdims=True) * (1.0 / tops)
                mid = mid.astype(BF16)
                centre[c] = (mid, mid.astype(F32))
            lefts[c].append(x.astype(BF16))
            rights[c].append(jnp.concatenate(main + [jnp.where(kept[c], edge, 0.0)], axis=1).astype(BF16))
            valid[c].append(edge[:, flag + c : flag + c + 1])
            out.append(jnp.sum(x * centre[c][1], axis=1, keepdims=True))
        return out

    def gram(b, lean):
        rows = []
        wide = -(-(b + 1) * STEP // LANES) * LANES
        for c in range(OWNED):
            mid, midf = centre[c]
            left = jnp.concatenate([lefts[c][b], jnp.broadcast_to(mid, (16, mid.shape[1])), sign[c]], axis=0)
            right = jnp.concatenate(rights[c], axis=0)
            if right.shape[0] < wide:
                right = jnp.concatenate([right, jnp.zeros((wide - right.shape[0], right.shape[1]), BF16)], axis=0)
            g = dot_t(left, right)
            along, has = g[STEP : STEP + 1], g[STEP + 16 : STEP + 17]
            along = along - jnp.sum(midf * midf) * has
            rows.append(g[:STEP] - valid[c][b] * along - lean[c] * has)
        return rows

    def scale(b, rows):
        wide = rows[0].shape[1]
        wl = lax.broadcasted_iota(jnp.int32, (STEP, wide), 1)
        ws = lax.broadcasted_iota(jnp.int32, (STEP, wide), 0)
        diag = wl == ws + b * STEP
        return [m + jnp.where(diag, number[c] * RIDGE, 0.0) for c, m in enumerate(rows)]

    def fetch(b):
        for r in range(max(b * span, 1), (b + 1) * span):
            go(r).wait_recv()
        return load(b)

    def measure(c):
        def run():
            lib = [held["lib"][: full * LANES]]
            lib += [held["lib"][full * LANES :] if i == c else jnp.zeros((rest, total), BF16) for i in range(OWNED)]
            lib += [jnp.zeros((pad, total), BF16)]
            u = dot_n(jnp.concatenate(lefts[c], axis=0), jnp.concatenate(lib, axis=0))
            v = jnp.concatenate(valid[c], axis=0)
            u = (u - jnp.sum(u, axis=0, keepdims=True) * (1.0 / number[c])) * v
            held[c] = jnp.concatenate([u, jnp.broadcast_to(v, (size, LANES))], axis=1)

        return run

    def advance(c):
        def run():
            u1, u2 = halves(held[c])
            m1, m2 = halves(jnp.concatenate([state.inverse[c][: size - STEP], held["maps"][c]], axis=0))
            z = dot_n(jnp.concatenate([m1, m1, m2], axis=1), jnp.concatenate([u1, u2, u1], axis=0))
            held["z", c] = z[: size - STEP]
            held["q", c] = z[size - STEP :]

        return run

    def summarise(c):
        def run():
            z = held["z", c]
            held["lib", c] = jnp.sum(held[c][: size - STEP] * z, axis=0, keepdims=True)
            held["sum", c] = jnp.sum(z, axis=0, keepdims=True)
            inv = state.inverse[c]
            held["diag", c] = [
                jnp.sum(jnp.where(diag, inv[i : i + LANES, i : i + LANES], 0.0), axis=1, keepdims=True)
                for i in range(0, size, LANES)
            ]

        return run

    def squares():
        tf = held["lib"].astype(F32)
        held["norm"] = jnp.sum(tf * tf, axis=0, keepdims=True)

    diag = lax.broadcasted_iota(jnp.int32, (LANES, LANES), 0) == lax.broadcasted_iota(jnp.int32, (LANES, LANES), 1)
    rows = gram(0, fetch(0))
    for r in range(1, devices):
        tell(r).wait_recv()
    heads = jnp.maximum(jnp.sum(heard[...], axis=0), 1.0)
    number = [heads[:, c * STEP : c * STEP + 1] for c in range(OWNED)]
    def prefetch(b):
        held["rows"] = gram(b, fetch(b))

    for b in range(blocks):
        pair, maps = state.reduce(scale(b, rows))
        if b < blocks - 1:
            hold = [lambda: None] * 11
            factor = paired_factor(pair, hold + [functools.partial(prefetch, b + 1)])
            state.extend(factor, maps)
            rows = held["rows"]
            if not b:
                lends[1].wait_recv()
                lends[2].start()
    held["maps"] = maps
    for i in (0, 2):
        lends[i].wait_recv()
    held["lib"] = jnp.concatenate([library[i] for i in range(n_grp)], axis=1)
    state.inverse = [grow(m, size, size) for m in state.inverse]
    fill = [measure(0), measure(1), squares, advance(0), advance(1), summarise(0), summarise(1)]
    factor = paired_factor(pair, fill)

    f1, f2 = halves(factor)
    left = jnp.concatenate([f1, f1, f2], axis=1)
    res = []
    for c in range(OWNED):
        n = number[c]
        m1, m2 = halves(jnp.concatenate([held["q", c], maps[c]], axis=1))
        both = dot_n(left, jnp.concatenate([pair_rows(t, c) for t in (m1, m2, m1)], axis=0))
        gu, g = both[:STEP, : total + LANES], both[:STEP, total + LANES :]
        nu, d = both[STEP:, : total + LANES], both[STEP:, total + LANES :]
        g1, g2 = halves(g)
        n1, n2 = halves(nu)
        z = dot_0(jnp.concatenate([g1, g1, g2], axis=0), jnp.concatenate([n1, n2, n1], axis=0))
        z = jnp.concatenate([held["z", c] + z[: size - STEP], z[size - STEP :]], axis=0)
        energy = held["lib", c] + jnp.sum(gu * nu, axis=0, keepdims=True)
        w = held["sum", c][:, :total] + jnp.sum(
            jnp.concatenate([gu[:, total:]] * (total // LANES), axis=1) * nu[:, :total], axis=0, keepdims=True
        )
        kd = thirds(g * d)
        kd = dot_0(jnp.concatenate(kd, axis=0), jnp.ones((3 * STEP, LANES), BF16))
        kd = kd + jnp.concatenate(held["diag", c], axis=0)
        p = z[:, total:]
        s = energy[:, total:]
        s = jnp.where(s > 0.0, 1.0 / jnp.where(s > 0.0, s, 1.0), 0.0)
        ws = w * s[:, 0:1]
        lib = (held["norm"] - energy[:, :total] + w * ws) * (1.0 / RIDGE)
        lib = 1.0 / (jnp.maximum(lib, 0.0) + EPS)
        kd = kd - p * p * s
        pix = n * (1.0 - (n * RIDGE) * kd) - 1.0
        gain = (n * n * bands) / (jnp.maximum(pix, 0.0) + EPS)
        pieces = []
        for i in range(0, total, LANES):
            e = z[:, i : i + LANES] - p * ws[:, i : i + LANES]
            pieces.append(e * e * gain * lib[:, i : i + LANES])
        res.append(jnp.concatenate(pieces, axis=1).reshape(devices, 1, CAP, total))
    joined = jnp.concatenate(res, axis=1).reshape(devices, OWNED * CAP, total).astype(BF16)
    outbound[...] = joined
    for i in range(half):
        back(half + i).start()
        if i:
            back(i).start()
    returned[0] = outbound[0]
    for r in range(1, devices):
        tell(r).wait_send()
        go(r).wait_send()
    for cp in lends:
        cp.wait_send()
    for r in range(1, devices):
        back(r).wait()
    out_ref[...] = dot_n(take_ref[...], returned[...].reshape(size * OWNED, total)).astype(BF16)


def narrow(pixels, labels, targets):
    n_tile, n_grp = lax.axis_size("tile"), lax.axis_size("grp")
    devices = n_tile * n_grp
    rows, bands = pixels.shape
    total = targets.shape[0] * n_grp
    deep = (OWNED * (bands // LANES) + 1) * SUB
    vmem = pl.BlockSpec(memory_space=pltpu.VMEM)
    dma = pltpu.SemaphoreType.DMA
    return pl.pallas_call(
        functools.partial(step_body, bands, n_tile, n_grp),
        out_shape=jax.ShapeDtypeStruct((rows, total), BF16),
        in_specs=[pl.BlockSpec(memory_space=pl.ANY)] * 3,
        out_specs=vmem,
        scratch_shapes=[
            pltpu.VMEM((1, rows), labels.dtype),
            pltpu.VMEM((bands, rows), BF16),
            pltpu.VMEM((bands, targets.shape[0]), BF16),
            pltpu.VMEM((devices, deep, LANES), BF16),
            pltpu.VMEM((devices, deep, LANES), BF16),
            pltpu.VMEM((devices, 1, LANES), F32),
            pltpu.VMEM((devices, 1, LANES), F32),
            pltpu.VMEM((n_grp, bands, targets.shape[0]), BF16),
            pltpu.VMEM((devices, OWNED * CAP, total), BF16),
            pltpu.VMEM((devices, OWNED * CAP, total), BF16),
            pltpu.VMEM((rows, NCLUST * CAP), BF16),
            dma((3,)),
            dma((devices,)), dma((devices,)),
            dma((devices,)), dma((devices,)),
            dma((n_grp,)), dma((n_grp,)),
            dma((devices,)), dma((devices,)),
        ],
        compiler_params=pltpu.CompilerParams(
            collective_id=0, has_side_effects=True, vmem_limit_bytes=60 * 1024 * 1024
        ),
    )(labels.reshape(1, rows), pixels.T, targets.T)


def wide_cluster(pixels, labels, targets):
    n_tile = lax.axis_size("tile")
    n_grp = lax.axis_size("grp")
    band_count = pixels.shape[1]
    per_owner = 2 * NCLUST // n_tile
    target_total = targets.shape[0] * n_grp
    clusters = jnp.arange(NCLUST, dtype=jnp.int32)
    member = (labels[:, None] == clusters[None, :]).astype(jnp.int32)
    local_count = jnp.sum(member, axis=0).astype(jnp.float32)
    counts = lax.psum(local_count, ("tile", "grp"))
    place_rank = jnp.sum(jnp.cumsum(member, axis=0) * member, axis=1) - 1
    owner_pair = labels // per_owner
    inner_slot = labels % per_owner
    slot_width = CAP
    target_tile = 2 * owner_pair
    slot_index = (target_tile * per_owner + inner_slot) * slot_width + place_rank
    slot_total = n_tile * per_owner * slot_width
    outgoing = jnp.zeros((slot_total, band_count), jnp.bfloat16).at[slot_index].set(pixels)
    outgoing = outgoing.reshape(n_tile, per_owner * slot_width, band_count)
    arrived = lax.all_to_all(outgoing, "tile", split_axis=0, concat_axis=0, tiled=True)
    grouped = arrived.reshape(n_tile, per_owner, slot_width, band_count)
    gram_sum = jnp.einsum("scwb,scwd->cbd", grouped, grouped, preferred_element_type=jnp.float32)
    first_sums = jnp.sum(grouped, axis=(0, 2), dtype=jnp.float32)
    gram_sum, first_sums = lax.psum((gram_sum, first_sums), "grp")
    own_pair = lax.axis_index("tile") // 2
    own_counts = lax.dynamic_slice_in_dim(counts, own_pair * per_owner, per_owner, 0)
    own_counts = jnp.maximum(own_counts, 1.0)
    centre = first_sums / own_counts[:, None]
    identity = jnp.eye(band_count, dtype=jnp.float32)
    covariance = (
        gram_sum / own_counts[:, None, None]
        - centre[:, :, None] * centre[:, None, :]
        + 0.05 * identity
    )
    factor = jnp.linalg.cholesky(covariance)
    inverse = jax.scipy.linalg.solve_triangular(
        factor, jnp.broadcast_to(identity, factor.shape), lower=True
    )
    whitened = jnp.einsum(
        "tb,cdb->ctd",
        lax.all_gather(targets, "grp", axis=0, tiled=True).astype(jnp.float32),
        inverse,
        precision=lax.Precision.HIGHEST,
    )
    lib_norm = jnp.sum(whitened * whitened, axis=-1)
    centered = grouped.astype(jnp.float32) - centre[None, :, None, :]
    white_pix = jnp.einsum("scwb,cdb->scwd", centered, inverse, precision=lax.Precision.HIGHEST)
    inner_prod = jnp.einsum("scwd,ctd->scwt", white_pix, whitened, precision=lax.Precision.HIGHEST)
    pix_norm = jnp.sum(white_pix * white_pix, axis=-1)
    result = (
        band_count
        * inner_prod
        * inner_prod
        / ((lib_norm[None, :, None, :] + 1e-06) * (pix_norm[:, :, :, None] + 1e-06))
    )
    outbound = result.astype(jnp.bfloat16).reshape(n_tile, per_owner * slot_width, target_total)
    returned = lax.all_to_all(outbound, "tile", split_axis=0, concat_axis=0, tiled=True)
    flat_scores = returned.reshape(slot_total, target_total)
    return flat_scores[slot_index]


def local(pixels, labels, targets):
    n_tile, n_grp = lax.axis_size("tile"), lax.axis_size("grp")
    devices = n_tile * n_grp
    rest = pixels.shape[1] % LANES
    if (
        NCLUST == OWNED * devices
        and n_grp == 4
        and n_tile & (n_tile - 1) == 0
        and devices * CAP % (2 * STEP) == 0
        and rest % 16 == 0
        and OWNED * (rest + 1) <= LANES
    ):
        return narrow(pixels, labels, targets)
    return wide_cluster(pixels, labels, targets)


def solution(mesh):
    return jax.shard_map(
        local,
        mesh=mesh,
        in_specs=(P(("tile", "grp"), None), P(("tile", "grp")), P("grp", None)),
        out_specs=P(("tile", "grp"), None),
        check_vma=False,
    )
```
